32 devices in a mesh: dp: 8 (over z, y), tensor: 4 (over x, core).
Axes of the slice: x: 2, y: 2, z: 4, core: 2. Of those that a mesh axis runs over, the one named last changes fastest.
Arguments:
- tokens: bfloat16 [8, 4, 512, 768], P(None, 'tensor', 'dp'), may hold values from -6 to 6
- cotangent: bfloat16 [8, 2048, 768], P('dp', 'tensor'), may hold values from -6 to 6
- lengths: int32 [8], replicated, may hold values from 1 to 2048, 12288 in all
- dealt_to: int32 [8], replicated, may hold values from 0 to 7, each once
- adapter_id: int32 [8], replicated, may hold values from 0 to 7
- norm_gain: bfloat16 [768], replicated, may hold values from 0.25 to 1.75
- w_zx: bfloat16 [768, 2, 1536], P('dp', None, 'tensor'), may hold values from -0.21875 to 0.21875
- w_dt: bfloat16 [768, 24], P('dp', 'tensor'), may hold values from -0.21875 to 0.21875
- w_bc: bfloat16 [768, 256], P('dp'), may hold values from -0.21875 to 0.21875
- x_kernel: float32 [4, 1536], P(None, 'tensor'), may hold values from -3 to 3
- x_offset: float32 [1536], P('tensor'), may hold values from -0.5 to 0.5
- bc_kernel: float32 [4, 256], replicated, may hold values from -3 to 3
- bc_offset: float32 [256], replicated, may hold values from -0.5 to 0.5
- dt_bias: float32 [24], P('tensor'), may hold values from -6.9 to -2.3
- a_log: float32 [24], P('tensor'), may hold values from 0 to 2.77
- d_skip: float32 [24], P('tensor'), may hold values from 0.5 to 1.5
- out_gain: bfloat16 [1536], P('tensor'), may hold values from 0.25 to 1.75
- w_out: bfloat16 [1536, 768], P('tensor', 'dp'), may hold values from -0.15625 to 0.15625
- inlet_down: bfloat16 [8, 768, 16], replicated, may hold values from -0.21875 to 0.21875
- inlet_up: bfloat16 [8, 16, 2, 1536], P(None, None, None, 'tensor'), may hold values from -1.5 to 1.5
- outlet_down: bfloat16 [8, 1536, 16], replicated, may hold values from -0.15625 to 0.15625
- outlet_up: bfloat16 [8, 16, 768], replicated, may hold values from -1.5 to 1.5
Outputs:
- output: bfloat16 [8, 2048, 768], P('dp', 'tensor')
- token_grads: bfloat16 [8, 4, 512, 768], P(None, 'tensor', 'dp')
- inlet_dgrad: float32 [8, 768, 16], replicated
- inlet_ugrad: float32 [8, 16, 2, 1536], P(None, None, None, 'tensor')
- outlet_dgrad: float32 [8, 1536, 16], replicated
- outlet_ugrad: float32 [8, 16, 768], replicated
The draws below stay inside these ranges and needn't reach their ends.
Inputs may be any that keep to these rules, and one draw needn't show every extreme that they name: `lengths`: the longest sequence has exactly 2048 positions. `dealt_to`: every group is named by exactly one sequence.
All inputs are finite; a program needn't handle non-finite values.
Results may differ from the reference program's by a relative error of at most 0.0085.
Values may be sent and summed in bfloat16 or wider, within the bound.
A program may use at most 128 MiB of HBM per device.

```python
import math
from functools import partial
import jax
import jax.numpy as jnp
import numpy as np
from jax import lax

D = 768
HEADS = 24
HEAD_DIM = 64
STATE = 128
INNER = 1536
CONV = 4
SPAN = 256
ADAPTERS = 8
RANK = 16
TOK_DEV = 512
SEQS = 8
STRETCHES = 4
LEN = 2048


def place_ends(values, rng, smallest, top_value):
    spot = [jax.random.randint(jax.random.fold_in(rng, axis), (), 0, length) for axis, length in enumerate(values.shape)]
    main_axis = values.shape.index(max(values.shape))
    beside = spot[:main_axis] + [(spot[main_axis] + 1) % values.shape[main_axis]] + spot[main_axis + 1:]
    return values.at[tuple(spot)].set(smallest).at[tuple(beside)].set(top_value)


def block_levels(rng, shape, pieces, least, high):
    level = 1.0
    for dim, shards_of in pieces:
        steps = jax.random.uniform(jax.random.fold_in(jax.random.fold_in(rng, 6), dim), (shards_of,), jnp.float32, least / len(pieces), high / len(pieces))
        level = level * jnp.repeat(jnp.exp(steps), shape[dim] // shards_of).reshape((-1,) + (1,) * (len(shape) - 1 - dim))
    return level


def length_profile(amount, total, most, skew):
    portions = [(1 << 20) // math.isqrt(standing ** skew) + 1 for standing in range(2, amount + 1)]
    rest, holding = total - most - (amount - 1), [1] * (amount - 1)
    while rest > 0:
        candidates = [i for i in range(amount - 1) if holding[i] < most]
        pool, budget = sum([portions[i] for i in candidates]), rest
        for i in candidates:
            extra = min(most - holding[i], max(1, budget * portions[i] // pool), rest)
            holding[i] = holding[i] + extra
            rest = rest - extra
    return np.array([most] + holding)


def ragged(rng, number_of, total, limit, lean):
    if number_of == 2:
        one = jax.random.randint(rng, (), max(1, total - limit), min(limit, total - 1) + 1)
        return jnp.stack([one, total - one])
    sizes = jnp.asarray(length_profile(number_of, total, limit, lean), jnp.int32)
    twos = (number_of - 1) // 2
    giver, taker = sizes[1:1 + 2 * twos:2], sizes[2:2 + 2 * twos:2]
    room = jnp.minimum(giver - 1, limit - taker)
    passed = jax.random.randint(jax.random.fold_in(rng, 1), (twos,), 0, 1 << 20) % (room + 1)
    sizes = sizes.at[1:1 + 2 * twos:2].set(giver - passed).at[2:2 + 2 * twos:2].set(taker + passed)
    return sizes[jax.random.permutation(jax.random.fold_in(rng, 2), number_of)]


def centred(rng, shape, scale, bound, split=(), kind=jnp.bfloat16):
    loudness = block_levels(rng, shape, split, -0.22, 0.18) if split else 1.0
    drawn = jax.random.normal(rng, shape, jnp.float32) * scale * loudness
    return jnp.minimum(jnp.maximum(drawn, -bound), bound).astype(kind)


def setup_inputs(seed: int = 0) -> dict:
    arg_keys = jax.random.split(jax.random.key(seed), 23)
    return {
        "tokens": centred(arg_keys[0], (SEQS, STRETCHES, TOK_DEV, D), 1.0, 6.0, ((1, 4), (2, 8))),
        "cotangent": centred(arg_keys[1], (SEQS, LEN, D), 1.0, 6.0, ((0, 8), (1, 4))),
        "lengths": ragged(arg_keys[2], SEQS, SEQS * LEN * 3 // 4, LEN, 2).astype(jnp.int32),
        "dealt_to": jax.random.permutation(arg_keys[3], SEQS).astype(jnp.int32),
        "adapter_id": place_ends(jax.random.randint(arg_keys[4], (SEQS,), 0, ADAPTERS), jax.random.fold_in(arg_keys[4], 1), 0, ADAPTERS - 1).astype(jnp.int32),
        "norm_gain": jnp.clip(1.0 + 0.15 * jax.random.normal(arg_keys[5], (D,), jnp.float32), 0.25, 1.75).astype(jnp.bfloat16),
        "w_zx": centred(arg_keys[6], (D, 2, INNER), D ** -0.5, 0.21875, ((0, 8), (2, 4))),
        "w_dt": centred(arg_keys[7], (D, HEADS), D ** -0.5, 0.21875, ((0, 8), (1, 4))),
        "w_bc": centred(arg_keys[8], (D, 2 * STATE), D ** -0.5, 0.21875, ((0, 8),)),
        "x_kernel": centred(arg_keys[9], (CONV, INNER), CONV ** -0.5, 3.0, ((1, 4),), jnp.float32),
        "x_offset": jnp.clip(jax.random.uniform(arg_keys[10], (INNER,), jnp.float32, -0.5, 0.5) * block_levels(arg_keys[10], (INNER,), ((0, 4),), -0.4, 0.0), -0.5, 0.5),
        "bc_kernel": centred(arg_keys[11], (CONV, 2 * STATE), CONV ** -0.5, 3.0, (), jnp.float32),
        "bc_offset": jnp.clip(jax.random.uniform(arg_keys[12], (2 * STATE,), jnp.float32, -0.5, 0.5), -0.5, 0.5),
        "dt_bias": jnp.clip(-6.9 + 4.6000001430511475 * jax.random.uniform(arg_keys[13], (HEADS,), jnp.float32) ** block_levels(arg_keys[13], (HEADS,), ((0, 4),), -0.2, 0.2), -6.9, -2.3),
        "a_log": jnp.clip(2.77 * jax.random.uniform(arg_keys[14], (HEADS,), jnp.float32) ** block_levels(arg_keys[14], (HEADS,), ((0, 4),), -0.2, 0.2), 0.0, 2.77),
        "d_skip": jnp.clip(0.5 + 1.0 * jax.random.uniform(arg_keys[15], (HEADS,), jnp.float32) ** block_levels(arg_keys[15], (HEADS,), ((0, 4),), -0.2, 0.2), 0.5, 1.5),
        "out_gain": jnp.clip(1.0 + 0.15 * jax.random.normal(arg_keys[16], (INNER,), jnp.float32), 0.25, 1.75).astype(jnp.bfloat16),
        "w_out": centred(arg_keys[17], (INNER, D), INNER ** -0.5, 0.15625, ((0, 4), (1, 8))),
        "inlet_down": centred(arg_keys[18], (ADAPTERS, D, RANK), D ** -0.5, 0.21875),
        "inlet_up": centred(arg_keys[19], (ADAPTERS, RANK, 2, INNER), RANK ** -0.5, 1.5, ((3, 4),)),
        "outlet_down": centred(arg_keys[20], (ADAPTERS, INNER, RANK), INNER ** -0.5, 0.15625),
        "outlet_up": centred(arg_keys[21], (ADAPTERS, RANK, D), RANK ** -0.5, 1.5),
    }


EPSILON = 1e-05
HIGHEST = lax.Precision.HIGHEST

@jax.custom_vjp
def low(v):
    return lax.optimization_barrier(v.astype(jnp.bfloat16)).astype(jnp.float32)

@jax.custom_vjp
def low_back(v):
    return v

def low_keep(v):
    return (low(v), None)

def low_pass(kept, grad):
    return (grad,)

def back_keep(v):
    return (v, None)

def back_low(kept, grad):
    return (low(grad),)
low.defvjp(low_keep, low_pass)
low_back.defvjp(back_keep, back_low)

def causal_conv(values, kernel, offsets):
    kernel_width = kernel.shape[0]
    length = values.shape[0]
    padded = jnp.pad(values, ((kernel_width - 1, 0), (0, 0)))
    running = jnp.zeros_like(values) + offsets[None, :]
    for offset in range(kernel_width):
        running = running + kernel[offset][None, :] * padded[offset:offset + length]
    return running

def span_step(decay_rates, state_now, block_in):
    block_x, block_dt, block_b, block_c = block_in
    log_decay = block_dt * decay_rates[None, :]
    within = jnp.cumsum(log_decay, axis=0)
    scores = jnp.dot(block_c, block_b.T, precision=HIGHEST, preferred_element_type=jnp.float32)
    span_len = block_x.shape[0]
    causal = (jnp.arange(span_len)[:, None] >= jnp.arange(span_len)[None, :])[:, :, None]
    spread = within[:, None, :] - within[None, :, :]
    mixing = jnp.where(causal, jnp.exp(jnp.where(causal, spread, 0.0)), 0.0)
    weights = scores[:, :, None] * mixing * block_dt[None, :, :]
    inside = jnp.einsum('tsh,shp->thp', weights, block_x, precision=HIGHEST)
    carried = jnp.einsum('tn,hpn->thp', block_c, state_now, precision=HIGHEST) * jnp.exp(within)[:, :, None]
    tail_weight = jnp.exp(within[-1][None, :] - within) * block_dt
    fresh_state = jnp.einsum('th,thp,tn->hpn', tail_weight, block_x, block_b, precision=HIGHEST)
    state_next = jnp.exp(within[-1])[:, None, None] * state_now + fresh_state
    return (state_next, inside + carried)

def scan_mixer(heads_x, step_size, decay_rates, input_b, input_c):
    blocks = heads_x.shape[0] // SPAN

    def spanned(tensor_in):
        return tensor_in.reshape((blocks, SPAN) + tensor_in.shape[1:])
    initial = jnp.zeros((heads_x.shape[1], heads_x.shape[2], input_b.shape[1]), jnp.float32)
    final_state, outputs = lax.scan(jax.checkpoint(partial(span_step, decay_rates)), initial, (spanned(heads_x), spanned(step_size), spanned(input_b), spanned(input_c)))
    return outputs.reshape(heads_x.shape)

def reference(tokens, cotangent, lengths, dealt_to, adapter_id, norm_gain, w_zx, w_dt, w_bc, x_kernel, x_offset, bc_kernel, bc_offset, dt_bias, a_log, d_skip, out_gain, w_out, inlet_down, inlet_up, outlet_down, outlet_up):
    seq_rows = tokens.astype(jnp.float32).reshape(SEQS, LEN, D)
    cot_rows = jnp.take(cotangent.astype(jnp.float32), dealt_to, axis=0)
    gain_in = norm_gain.astype(jnp.float32)
    gain_out = out_gain.astype(jnp.float32)
    proj_zx = w_zx.astype(jnp.float32).reshape(D, 2 * INNER)
    proj_dt = w_dt.astype(jnp.float32)
    proj_bc = w_bc.astype(jnp.float32)
    proj_out = w_out.astype(jnp.float32)
    decay_rates = -jnp.exp(a_log)
    adapters = (inlet_down.astype(jnp.float32), inlet_up.astype(jnp.float32).reshape(ADAPTERS, RANK, 2 * INNER), outlet_down.astype(jnp.float32), outlet_up.astype(jnp.float32))
    positions = jnp.arange(LEN, dtype=jnp.int32)

    def block_layer(onehot_row, valid_rows, residual, adapter_set):
        down_in, up_in, down_out, up_out = [jnp.einsum('k,kab->ab', onehot_row, stacked, precision=HIGHEST) for stacked in adapter_set]
        mean_sq = lax.optimization_barrier(jnp.mean(residual * residual, axis=1, keepdims=True))
        normed = low(residual * lax.rsqrt(mean_sq + EPSILON) * gain_in)
        hidden_in = low_back(low(jnp.dot(normed, down_in, precision=HIGHEST, preferred_element_type=jnp.float32)))
        p_zx = low_back(jnp.dot(normed, proj_zx, precision=HIGHEST, preferred_element_type=jnp.float32) + jnp.dot(hidden_in, up_in, precision=HIGHEST, preferred_element_type=jnp.float32))
        p_bc = low_back(jnp.dot(normed, proj_bc, precision=HIGHEST, preferred_element_type=jnp.float32))
        p_dt = low_back(jnp.dot(normed, proj_dt, precision=HIGHEST, preferred_element_type=jnp.float32))
        inner_x = jax.nn.silu(causal_conv(p_zx[:, INNER:], x_kernel, x_offset))
        mixed_bc = jax.nn.silu(causal_conv(p_bc, bc_kernel, bc_offset))
        step_size = jax.nn.softplus(p_dt + dt_bias)
        heads_x = inner_x.reshape(LEN, HEADS, HEAD_DIM)
        ssm_out = scan_mixer(heads_x, step_size, decay_rates, mixed_bc[:, :STATE], mixed_bc[:, STATE:]) + d_skip[None, :, None] * heads_x
        gated_act = ssm_out.reshape(LEN, INNER) * jax.nn.silu(p_zx[:, :INNER])
        mean_g = lax.optimization_barrier(jnp.mean(gated_act * gated_act, axis=1, keepdims=True))
        normed_out = low(gated_act * lax.rsqrt(mean_g + EPSILON) * gain_out)
        hidden_out = low_back(low(jnp.dot(normed_out, down_out, precision=HIGHEST, preferred_element_type=jnp.float32)))
        branch_out = low_back(jnp.dot(normed_out, proj_out, precision=HIGHEST, preferred_element_type=jnp.float32) + jnp.dot(hidden_out, up_out, precision=HIGHEST, preferred_element_type=jnp.float32))
        return residual + valid_rows[:, None] * branch_out

    def per_sequence(totals, seq_item):
        residual, cot_seq, length, adapter_no = seq_item
        onehot_row = (jnp.arange(ADAPTERS, dtype=jnp.int32) == adapter_no).astype(jnp.float32)
        valid_rows = (positions < length).astype(jnp.float32)
        result, pull_back = jax.vjp(partial(block_layer, onehot_row, valid_rows), residual, adapters)
        grad_res, grad_adapt = pull_back(cot_seq)
        totals = jax.tree.map(lambda running_sum, fresh_grad: running_sum + fresh_grad, totals, grad_adapt)
        return (totals, (result.astype(jnp.bfloat16), grad_res.astype(jnp.bfloat16)))
    initial = jax.tree.map(jnp.zeros_like, adapters)
    totals, (out_rows, grad_rows) = lax.scan(per_sequence, initial, (seq_rows, cot_rows, lengths, adapter_id))
    output = jnp.zeros_like(out_rows).at[dealt_to].set(out_rows)
    token_grads = grad_rows.reshape(SEQS, STRETCHES, TOK_DEV, D)
    return (output, token_grads, totals[0], totals[1].reshape(ADAPTERS, RANK, 2, INNER), totals[2], totals[3])
```

```python
from functools import partial
from types import SimpleNamespace

import jax
import jax.numpy as jnp
from jax import lax
from jax.experimental import pallas as pl
from jax.experimental.pallas import tpu as pltpu
from jax.sharding import PartitionSpec as P

EPSILON = 1e-05
LOG2E = 1.4426950408889634
HIGHEST = lax.Precision.HIGHEST
MESH = pl.DeviceIdType.MESH
f32, bf16 = jnp.float32, jnp.bfloat16

BLOCKS = 4
WIDE = 384
HEADS_B = 6
SLOT = 16
CHUNK = 128
HALO = 16
ADAPTERS = 8
TOK_AT = 2
LOADED = (
    "w_zx",
    "w_dt_in",
    "x_kernel",
    "x_offset",
    "out_gain",
    "dt_bias",
    "a_log",
    "d_skip",
    "inlet_up",
    "tokens",
    "cot",
    "gain",
    "bc_kernel",
    "bc_offset",
    "inlet_down",
    "outlet_up",
    "outlet_down",
)


def nn(a, b):
    return jnp.dot(a, b, preferred_element_type=f32)


def nt(a, b):
    return lax.dot_general(a, b, (((1,), (1,)), ((), ())), preferred_element_type=f32)


def tn(a, b):
    return lax.dot_general(a, b, (((0,), (0,)), ((), ())), preferred_element_type=f32)


def two_part(v):
    high = v.astype(bf16)
    return jnp.concatenate([high, (v - high.astype(f32)).astype(bf16)], axis=1)


def sigmoid(v):
    return 1.0 / (1.0 + jnp.exp(-v))


def thirds(v):
    return v[:, :128] + v[:, 128:256] + v[:, 256:384]


def loop(count, body):
    lax.fori_loop(0, count, lambda i, carry: (body(i), carry)[1], 0)


def remote(src, dst, ssem, rsem, peer):
    return pltpu.make_async_remote_copy(src, dst, ssem, rsem, device_id=peer, device_id_type=MESH)


class Spread:
    def __init__(self, buf, ssem, rsem, piece, dp, tp, dp_size, all_blocks):
        self.buf, self.ssem, self.rsem, self.piece = buf, ssem, rsem, piece
        self.dp, self.tp, self.nz, self.n = dp, tp, dp_size // 2, dp_size
        self.z, self.y = lax.div(dp, 2), lax.rem(dp, 2)
        self.all_blocks = all_blocks
        self.core = tp + 1 - 2 * lax.rem(tp, 2)
        self.far = lax.rem(tp + 2, 4)
        self.far_core = lax.rem(self.core + 2, 4)

    def at(self, t, d):
        rows = pl.ds(pl.multiple_of(d * self.piece, 16), self.piece)
        return self.buf.at[t, rows, :] if self.all_blocks else self.buf.at[rows, :]

    def copy(self, kind, t, d):
        peer = (
            (jnp.minimum(self.dp + 2, self.n - 1), self.tp),
            (jnp.maximum(self.dp - 2, 0), self.tp),
            (self.dp + 1 - 2 * self.y, self.tp),
            (self.dp, self.far),
            (self.dp, self.core),
            (self.dp, self.core),
        )[kind]
        rsem = self.rsem.at[t, d] if self.all_blocks else self.rsem.at[d]
        return remote(self.at(t, d), self.at(t, d), self.ssem.at[kind, d], rsem, peer)

    def wait(self, t, d):
        self.copy(2, t, d).wait_recv()

    def sideways(self, d):
        self.copy(2, self.tp, d).start()
        self.across(d)

    def across(self, d):
        if self.all_blocks:
            self.copy(3, self.tp, d).start()

    def column(self, t):
        peer = (self.dp, self.core)
        return remote(self.buf.at[t], self.buf.at[t], self.ssem.at[4, 0], self.rsem.at[t, 0], peer)

    def begin(self):
        @pl.when(self.z < self.nz - 1)
        def _():
            self.copy(0, self.tp, self.dp).start()

        @pl.when(self.z > 0)
        def _():
            self.copy(1, self.tp, self.dp).start()

        self.sideways(self.dp)

    def hop(self, k):
        low, high = self.dp - 2 * k, self.dp + 2 * k

        @pl.when(self.z >= k)
        def _():
            self.wait(self.tp, low)

            @pl.when(self.z < self.nz - 1)
            def _():
                self.copy(0, self.tp, low).start()

            self.sideways(low)

        @pl.when(self.z + k < self.nz)
        def _():
            self.wait(self.tp, high)

            @pl.when(self.z > 0)
            def _():
                self.copy(1, self.tp, high).start()

            self.sideways(high)

    def from_y(self, k):
        other = 1 - 2 * self.y
        low, high = self.dp + other - 2 * k, self.dp + other + 2 * k

        @pl.when(self.z >= k)
        def _():
            self.wait(self.tp, low)
            self.across(low)

        if k:

            @pl.when(self.z + k < self.nz)
            def _():
                self.wait(self.tp, high)
                self.across(high)

    def own_done(self):
        self.column(self.tp).start()

    def from_x(self):
        def forward(d):
            self.wait(self.far, d)
            self.copy(5, self.far, d).start()

        other = 1 - 2 * self.y
        for k in range(self.nz + 1):
            for shift, reach in ((0, k), (other, k - 1)):
                low, high = self.dp + shift - 2 * reach, self.dp + shift + 2 * reach
                if 0 <= reach < self.nz:

                    @pl.when(self.z >= reach)
                    def _(low=low):
                        forward(low)

                    if reach:

                        @pl.when(self.z + reach < self.nz)
                        def _(high=high):
                            forward(high)

    def from_core(self):
        self.column(self.core).wait_recv()
        self.from_far_core()

    def from_far_core(self):
        for k in range(self.n):
            self.wait(self.far_core, lax.rem(self.dp + k, self.n))

    def finish(self):
        for zz in range(self.nz):
            d = 2 * zz + self.y

            @pl.when(jnp.logical_and(self.z >= zz, self.z < self.nz - 1))
            def _():
                self.copy(0, self.tp, d).wait_send()

            @pl.when(jnp.logical_and(self.z <= zz, self.z > 0))
            def _():
                self.copy(1, self.tp, d).wait_send()

            self.copy(2, self.tp, d).wait_send()
        if self.all_blocks:
            for d in range(self.n):
                self.copy(3, self.tp, d).wait_send()
                self.copy(5, self.far, d).wait_send()
            self.column(self.tp).wait_send()


class Toward:
    def __init__(self, me, size, peer, src, dst, ssem, rsem):
        self.me, self.size, self.peer = me, size, peer
        self.src, self.dst, self.ssem, self.rsem = src, dst, ssem, rsem

    def copy(self, to, sender):
        return remote(self.src(to), self.dst(sender), self.ssem.at[to], self.rsem.at[sender], self.peer(to))

    def others(self):
        return [lax.rem(self.me + k, self.size) for k in range(1, self.size)]

    def start(self):
        for to in self.others():
            self.copy(to, self.me).start()

    def wait(self):
        for sender in self.others():
            self.copy(sender, sender).wait_recv()

    def finish(self):
        for to in self.others():
            self.copy(to, self.me).wait_send()


def front(r, dp, tp, dp_size, tp_size, load, scalars, work):
    block = r.tok_out.shape[1]
    rows_n = r.gbr.shape[0]
    piece = r.w_dt_in.shape[1]
    own_rows = pl.ds(pl.multiple_of(piece * dp, 16), piece)

    def place(d):
        return pl.ds(pl.multiple_of(HALO + block * d, 16), block)

    r.dts[tp, dp] = jnp.zeros_like(r.dts[tp, dp])
    r.small[tp] = jnp.zeros_like(r.small[tp])
    r.wdt[...] = jnp.zeros_like(r.wdt)
    own_out = pltpu.make_async_copy(r.w_out, r.wout.at[tp, own_rows, :], r.own_sem.at[0])
    own_bc = pltpu.make_async_copy(r.w_bc, r.wbc.at[own_rows, :], r.own_sem.at[1])
    own_out.start()
    own_bc.start()
    load.wait("w_zx")
    for k in range(2):
        r.zx[tp, own_rows, k * WIDE : (k + 1) * WIDE] = r.w_zx[:, k, :]
    own_bc.wait()
    work.greet()

    def to_dp(d):
        return (d, tp)

    def to_tp(t):
        return (dp, t)

    zx = Spread(r.zx, r.zx_ss, r.zx_rs, piece, dp, tp, dp_size, True)
    wout = Spread(r.wout, r.wo_ss, r.wo_rs, piece, dp, tp, dp_size, True)
    wbc = Spread(r.wbc, r.bc_ss, r.bc_rs, piece, dp, tp, dp_size, False)
    tok = Toward(dp, dp_size, to_dp, lambda d: r.tok_out.at[d], lambda d: r.ext.at[place(d), :], r.tok_ss, r.tok_rs)
    dts = Toward(dp, dp_size, to_dp, lambda d: r.dts.at[tp, dp], lambda d: r.dts.at[tp, d], r.dt_ss, r.dt_rs)
    dts2 = Toward(tp, tp_size, to_tp, lambda t: r.dts.at[tp], lambda t: r.dts.at[t], r.d2_ss, r.d2_rs)
    ups = Toward(tp, tp_size, to_tp, lambda t: r.up.at[tp], lambda t: r.up.at[t], r.up_ss, r.up_rs)
    smalls = Toward(tp, tp_size, to_tp, lambda t: r.small.at[tp], lambda t: r.small.at[t], r.sm_ss, r.sm_rs)

    zx.begin()
    wbc.begin()
    load.wait("w_dt_in", "x_kernel", "x_offset", "out_gain", "dt_bias", "a_log", "d_skip", "inlet_up")
    r.dts[tp, dp, 0:HEADS_B, 0:piece] = r.w_dt_in[...]
    r.small[tp, 0:4, :] = r.x_kernel[...]
    r.small[tp, 4, :] = r.x_offset[...]
    r.small[tp, 5, :] = r.out_gain[...].astype(f32)
    r.small[tp, 6, 0:HEADS_B] = r.dt_bias[...]
    r.small[tp, 7, 0:HEADS_B] = r.a_log[...]
    r.small[tp, 8, 0:HEADS_B] = r.d_skip[...]
    adapter = scalars.adapter()
    for k in range(2):
        r.up[tp, :, k * WIDE : (k + 1) * WIDE] = r.inlet_up[adapter, :, k, :]
    dts.start()
    ups.start()
    smalls.start()
    load.wait("tokens")
    for g in range(dp_size):
        r.tok_out[g] = r.tokens[scalars.seq_of(g)]
    r.ext[place(dp), :] = r.tok_out[dp]
    for k in range(1, zx.nz):
        zx.hop(k)
        zx.from_y(k - 1)
        if k == TOK_AT:
            tok.start()
        wbc.hop(k)
        wbc.from_y(k - 1)
    dts.wait()
    dts2.start()
    zx.from_y(zx.nz - 1)
    zx.own_done()
    wbc.from_y(zx.nz - 1)
    own_out.wait()
    wout.begin()
    work.early()
    dts2.wait()
    ups.wait()
    smalls.wait()
    for d in range(dp_size):
        lines = jnp.concatenate([r.dts[t, d].astype(f32) for t in range(BLOCKS)] * 2, axis=0)
        r.wdt[d * piece : (d + 1) * piece, :] = lines.T[:piece].astype(bf16)
    tok.wait()
    edge = remote(
        r.ext.at[rows_n : rows_n + HALO, :],
        r.ext.at[0:HALO, :],
        r.ha_ss.at[0],
        r.ha_rs.at[0],
        (dp, lax.rem(tp + 1, tp_size)),
    )

    @pl.when(tp < tp_size - 1)
    def _():
        edge.start()

    work.norm_own()

    @pl.when(tp > 0)
    def _():
        edge.wait_recv()

    @pl.when(tp == 0)
    def _():
        r.ext[0:HALO, :] = jnp.zeros((HALO, r.ext.shape[1]), bf16)

    work.norm_edge()
    work.project(tp)
    zx.from_x()
    wout.hop(1)
    wout.from_y(0)
    zx.column(zx.core).wait_recv()
    work.project(zx.core)
    work.project_bc()
    wout.hop(2)
    wout.from_y(1)
    work.project(zx.far)
    zx.from_far_core()
    wout.hop(3)
    wout.from_y(2)
    wout.from_y(3)
    wout.own_done()
    work.project(zx.far_core)

    def end():
        for part in (zx, wbc, wout, tok, dts, dts2, ups, smalls):
            part.finish()

        @pl.when(tp < tp_size - 1)
        def _():
            edge.wait_send()

    return wout, end


class Returns:
    def __init__(self, r, dp, tp, dp_size):
        self.r, self.dp, self.tp, self.n = r, dp, tp, dp_size
        self.block = r.tok_out.shape[1]

    def rows(self, d):
        return pl.ds(pl.multiple_of(self.block * d, 16), self.block)

    def copy(self, d, sender):
        r = self.r
        return remote(r.tg.at[self.rows(d), :], r.tg_in.at[sender], r.tg_ss.at[d], r.tg_rs.at[sender], (d, self.tp))

    def own(self):
        r = self.r
        return pltpu.make_async_copy(r.tg.at[self.rows(self.dp), :], r.tg_in.at[self.dp], r.own_sem.at[2])

    def send(self, d):
        @pl.when(d != self.dp)
        def _():
            self.copy(d, self.dp).start()

        @pl.when(d == self.dp)
        def _():
            self.own().start()

    def others(self):
        return [lax.rem(self.dp + k, self.n) for k in range(1, self.n)]

    def finish(self):
        self.own().wait()
        for d in self.others():
            self.copy(d, d).wait_recv()
        for d in self.others():
            self.copy(d, self.dp).wait_send()


class Sums:
    def __init__(self, r, dp, tp, dp_size, tp_size, part):
        self.r, self.dp, self.tp, self.part = r, dp, tp, part

        def to_tp(t):
            return (dp, t)

        def to_dp(d):
            return (d, tp)

        sems = ((r.ga_ss, r.ga_rs), (r.gb_ss, r.gb_rs))[part]
        sends = ((r.gc_ss, r.gc_rs), (r.gd_ss, r.gd_rs))[part]
        dst = (r.all_up, r.all_rest)[part]
        self.first = Toward(tp, tp_size, to_tp, lambda t: r.sum_out.at[part, t], lambda t: r.sum_in.at[part, t], *sems)
        self.second = Toward(
            dp,
            dp_size,
            to_dp,
            lambda d: r.sum_all.at[part],
            lambda d: dst.at[d] if part == 0 else dst.at[tp, d],
            *sends,
        )
        self.own = pltpu.make_async_copy(
            r.sum_all.at[part], dst.at[dp] if part == 0 else dst.at[tp, dp], r.own_sem.at[3 + part]
        )
        self.core = tp + 1 - 2 * lax.rem(tp, 2)
        self.far = lax.rem(tp + 2, 4)

    def start(self):
        self.first.start()

    def middle(self):
        r, part = self.r, self.part
        r.sum_in[part, self.tp] = r.sum_out[part, self.tp]
        self.first.wait()
        total = r.sum_in[part, 0].astype(f32)
        for t in range(1, BLOCKS):
            total = total + r.sum_in[part, t].astype(f32)
        r.sum_all[part] = total.astype(bf16)
        self.second.start()
        self.own.start()

    def hop(self, kind, t, peer):
        rest = self.r.all_rest.at[t]
        return remote(rest, rest, self.r.g3_ss.at[kind], self.r.g3_rs.at[t], (self.dp, peer))

    def gathered(self):
        self.second.wait()
        self.own.wait()
        if self.part:
            self.hop(0, self.tp, self.far).start()
            self.hop(1, self.tp, self.core).start()

    def pass_on(self):
        self.hop(0, self.far, self.far).wait_recv()
        self.hop(2, self.far, self.core).start()

    def finish(self):
        if self.part:
            self.hop(1, self.core, self.core).wait_recv()
            self.hop(2, lax.rem(self.core + 2, 4), self.core).wait_recv()
            for kind, t in ((0, self.tp), (1, self.tp), (2, self.far)):
                self.hop(kind, t, self.core).wait_send()
        self.first.finish()
        self.second.finish()


class Loads:
    def __init__(self, r, names):
        self.copies = {}
        for i, name in enumerate(names):
            src, dst = getattr(r, name), getattr(r, "v_" + name)
            self.copies[name] = pltpu.make_async_copy(src, dst, r.load_sem.at[i])
            setattr(r, name, dst)

    def start(self):
        for copy in self.copies.values():
            copy.start()

    def wait(self, *names):
        for name in names:
            self.copies[name].wait()


def mixer_kernel(direct, names, *refs):
    r = SimpleNamespace(**dict(zip(names, refs)))
    dp, tp = lax.axis_index("dp"), lax.axis_index("tensor")
    tp_size = lax.axis_size("tensor")
    lengths, dealt, adapters = r.lengths, r.dealt_to, r.adapter_id
    rows_n = r.cot.shape[0]
    chunks = rows_n // CHUNK
    after, before = lax.rem(tp + 1, tp_size), lax.rem(tp + tp_size - 1, tp_size)

    dp_size = lax.axis_size("dp")
    barrier = pltpu.get_barrier_semaphore()
    peers = [(dp, after), (dp, before)]
    if direct:
        peers = [(dp, lax.rem(tp + k, tp_size)) for k in range(1, tp_size)]
        peers += [(lax.rem(dp + k, dp_size), tp) for k in range(1, dp_size)]
    for peer in peers:
        pl.semaphore_signal(barrier, inc=1, device_id=peer, device_id_type=MESH)

    def greet():
        pl.semaphore_wait(barrier, len(peers))

    def seq_of(g):
        seq = jnp.int32(0)
        for s in range(dealt.shape[0]):
            seq = jnp.where(dealt[s] == g, s, seq)
        return seq

    own = seq_of(dp)
    adapter, length = adapters[own], lengths[own]
    if direct:
        r.tg = r.gbr
        load = Loads(r, LOADED)
        load.start()
    else:
        r.out_rows = r.out
        greet()

    ext, nrm, hid, zx, up = r.ext, r.nrm, r.hid, r.zx, r.up
    gate, spz, px, xs, spx, xd = r.gate, r.spz, r.px, r.xs, r.spx, r.xd
    expand, small, pb, pd = r.expand, r.small, r.pb, r.pd
    dth, ech, tlh, eth, cu, cut, tot = r.dth, r.ech, r.tlh, r.eth, r.cu, r.cut, r.tot
    ub, bb, cb, bt, ct, sc = r.ub, r.bb, r.cb, r.bt, r.ct, r.sc
    st, rt, y, gy, gzx, xp = r.st, r.rt, r.y, r.gy, r.gzx, r.px

    def rows(c, base=0, size=CHUNK):
        return pl.ds(pl.multiple_of(c * CHUNK + base, 16), size)

    def valid(c):
        at = tp * rows_n + c * CHUNK + lax.broadcasted_iota(jnp.int32, (CHUNK, 1), 0)
        return jnp.where(at < length, 1.0, 0.0).astype(f32)

    def fill_expand(b):
        head = jnp.bitwise_and(lax.broadcasted_iota(jnp.int32, (256, WIDE), 0), 127)
        lane = lax.broadcasted_iota(jnp.int32, (256, WIDE), 1)
        expand[b] = jnp.where(head == SLOT * b + lax.shift_right_logical(lane, 6), 1.0, 0.0).astype(bf16)

    def take_adapter():
        r.idn[...] = r.inlet_down[adapter]
        r.oup[...] = r.outlet_up[adapter]
        for b in range(BLOCKS):
            r.odn[b] = r.outlet_down[adapter, :, b * WIDE : (b + 1) * WIDE]

    cot, gbr, ghid, wout = r.cot, r.gbr, r.ghid, r.wout

    def mask_cot(c):
        gbr[rows(c), :] = (cot[rows(c), :].astype(f32) * valid(c)).astype(bf16)

    def early():
        if direct:
            load.wait("cot", "gain", "bc_kernel", "bc_offset", "inlet_down", "outlet_up", "outlet_down")
        take_adapter()
        loop(BLOCKS, fill_expand)
        loop(chunks, mask_cot)
        ghid[...] = nt(gbr[...], r.oup[...]).astype(bf16)
        r.ghid_t[...] = nt(r.oup[...], gbr[...]).astype(bf16)

    def norm_rows(at, size):
        u = ext[pl.ds(at, size), :].astype(f32)
        inv = lax.rsqrt(jnp.mean(u * u, axis=1, keepdims=True) + EPSILON)
        nrm[pl.ds(at, size), :] = (u * inv * r.gain[...].astype(f32)[None]).astype(bf16)

    def norm_own():
        loop(chunks, lambda c: norm_rows(pl.multiple_of(c * CHUNK + HALO, 16), CHUNK))

    def norm_edge():
        norm_rows(0, HALO)
        hid[...] = nt(nrm[...], r.idn[...]).astype(bf16)

    def project(b):
        p = nn(nrm[...], zx[b]) + nn(hid[...], up[b])
        gate[b] = p[HALO:, :WIDE]
        px[b] = p[:, WIDE:]

    low_tri = lax.broadcasted_iota(jnp.int32, (CHUNK, CHUNK), 0) >= lax.broadcasted_iota(
        jnp.int32, (CHUNK, CHUNK), 1
    )

    def head_lanes():
        total = small[0, :, :128]
        for b in range(1, BLOCKS):
            total = total + pltpu.roll(small[b, :, :128], SLOT * b, 1)
        return total

    def steps(c):
        tri = jnp.where(low_tri, 1.0, 0.0).astype(f32)
        p = pd[rows(c), :]
        e = jnp.exp(-jnp.abs(p))
        log1p = jnp.where(e < 0.01, e * (1.0 - e * (0.5 - e * (1.0 / 3.0))), jnp.log(1.0 + e))
        dt = jnp.maximum(p, 0.0) + log1p
        rate = r.decay[0:1, :] * LOG2E
        cum = jnp.dot(tri, dt * rate, precision=HIGHEST, preferred_element_type=f32)
        total = cum[CHUNK - 1 : CHUNK]
        cu[rows(c), :] = cum
        cut[c] = cum.T
        tot[pl.ds(c, 1), :] = total
        dth[rows(c), :] = two_part(dt)
        ech[rows(c), :] = two_part(jnp.exp2(cum))
        tlh[rows(c), :] = two_part(jnp.exp2(total - cum))

    bc_kernel, bc_offset = r.bc_kernel, r.bc_offset

    def conv(window, kernel_row, offset):
        total = offset + kernel_row(3) * window[8:]
        for j in range(3):
            shifted = pltpu.roll(window, window.shape[0] - (5 + j), 0)
            total = total + kernel_row(j) * shifted[:CHUNK]
        return total

    def make_bc(c):
        window = pb[pl.ds(pl.multiple_of(c * CHUNK + 8, 8), CHUNK + 8), :]
        u = conv(window, lambda j: bc_kernel[j : j + 1, :], bc_offset[...][None])
        v = u * sigmoid(u)
        ub[rows(c), :] = u
        b_rows, c_rows = v[:, :128], v[:, 128:]
        bb[rows(c), :] = b_rows.astype(bf16)
        cb[rows(c), :] = c_rows.astype(bf16)
        bt[c] = b_rows.T.astype(bf16)
        ct[c] = c_rows.T.astype(bf16)
        sc[c] = jnp.where(low_tri, nt(c_rows.astype(bf16), b_rows.astype(bf16)), 0.0)

    def project_bc():
        head_rows = head_lanes()
        r.decay[...] = jnp.broadcast_to(-jnp.exp(head_rows[7:8]), (8, 128))
        r.skip[...] = two_part(head_rows)
        pb[...] = nn(nrm[...], r.wbc[...])
        pd[...] = nn(nrm[HALO:, :], r.wdt[...]) + head_rows[6:7]
        tot[...] = jnp.zeros_like(tot)
        loop(chunks, steps)
        tot[chunks : chunks + 1, :] = jnp.sum(tot[0:chunks, :], axis=0, keepdims=True)
        eth[...] = two_part(jnp.exp2(tot[...]))
        loop(chunks, make_bc)

    if direct:
        work = SimpleNamespace(
            greet=greet, early=early, norm_own=norm_own, norm_edge=norm_edge, project=project, project_bc=project_bc
        )
        scalars = SimpleNamespace(adapter=lambda: adapter, seq_of=seq_of)
        late, end_front = front(r, dp, tp, dp_size, tp_size, load, scalars, work)
    else:
        early()
        norm_own()
        norm_edge()
        loop(BLOCKS, project)
        project_bc()
    decay = r.decay[0:1, :]

    def make_x(b):
        def part(c):
            window = px[b, pl.ds(pl.multiple_of(c * CHUNK + 8, 8), CHUNK + 8), :]
            u = conv(window, lambda j: small[b, j : j + 1, :], small[b, 4:5, :])
            s = sigmoid(u)
            x = u * s
            xs[b, rows(c), :] = x
            spx[b, rows(c), :] = (s + x * (1.0 - s)).astype(bf16)
            xdt = x * nn(dth[rows(c), :], expand[b])
            xd[b, rows(c), :] = xdt.astype(bf16)
            st[c, b] = nn(bt[c], (xdt * nn(tlh[rows(c), :], expand[b])).astype(bf16))
            z = gate[b, rows(c), :]
            s = sigmoid(z)
            g = z * s
            gate[b, rows(c), :] = g
            spz[b, rows(c), :] = (s + g * (1.0 - s)).astype(bf16)

        loop(chunks, part)
        et = nn(eth[...], expand[b])
        r.et[b] = et
        r.skips[b] = nn(r.skip[...], expand[b])
        total = st[0, b]
        for c in range(1, chunks):
            total = total * et[c : c + 1] + st[c, b]
        r.fresh[b] = total

    loop(BLOCKS, make_x)
    if direct:
        late.from_x()

    class Chain:
        def __init__(self, src, dst, ssem, rsem, to, place):
            self.src, self.dst, self.ssem, self.rsem, self.to, self.place = src, dst, ssem, rsem, to, place

        def copy(self, b):
            return remote(self.src.at[b], self.dst.at[b], self.ssem.at[b], self.rsem.at[b], (dp, self.to))

        def begin(self):
            @pl.when(self.place == 0)
            def _():
                for b in range(BLOCKS):
                    self.src[b] = r.fresh[b].astype(bf16)
                    self.copy(b).start()
                    self.dst[b] = jnp.zeros_like(self.dst[b])

        def step(self, cond):
            @pl.when(cond)
            def _():
                for b in range(BLOCKS):
                    self.copy(b).wait_recv()

                    @pl.when(self.place < tp_size - 1)
                    def _(b=b):
                        grown = self.dst[b].astype(f32) * r.et[b][chunks : chunks + 1]
                        self.src[b] = (grown + r.fresh[b]).astype(bf16)
                        self.copy(b).start()

        def end(self):
            @pl.when(self.place < tp_size - 1)
            def _():
                for b in range(BLOCKS):
                    self.copy(b).wait_send()

    at_first, at_last = tp == 0, tp == tp_size - 1
    s_chain = Chain(r.s_out, r.s_in, r.s_ss, r.s_rs, after, tp)
    r_chain = Chain(r.r_out, r.r_in, r.r_ss, r.r_rs, before, tp_size - 1 - tp)
    s_chain.begin()

    half = lax.broadcasted_iota(jnp.int32, (CHUNK, 128), 1) < 64

    def pair_terms(b, c, i):
        lanes = slice(128 * i, 128 * (i + 1))
        cum = r.cub[rows(c), :]
        cols = jnp.concatenate(
            [jnp.broadcast_to(cum[:, 2 * i + k : 2 * i + k + 1], (CHUNK, CHUNK)) for k in range(2)], axis=1
        )
        line = jnp.concatenate([cut[c, pl.ds(SLOT * b + 2 * i + k, 1), :] for k in range(2)], axis=1)
        mixing = jnp.exp2(jnp.minimum(cols - line, 0.0))
        scores = sc[c]
        weights = (mixing * jnp.concatenate([scores, scores], axis=1)).astype(bf16)
        pair = xd[b, rows(c), lanes]
        none = jnp.zeros_like(pair)
        split = jnp.concatenate([jnp.where(half, pair, none), jnp.where(half, none, pair)], axis=0)
        return lanes, mixing, weights, split

    def turn_heads(b):
        for c in range(chunks):
            r.cub[rows(c), :] = pltpu.roll(cu[rows(c), :], lax.rem(128 - SLOT * b, 128), 1)

    def inside(b):
        turn_heads(b)

        def part(c):
            for i in range(HEADS_B // 2):
                lanes, mixing, weights, split = pair_terms(b, c, i)
                y[b, rows(c), lanes] = nn(weights, split)

        loop(chunks, part)
        s_chain.step(jnp.logical_and(b == 0, tp == 1))

    loop(BLOCKS, inside)
    if direct:
        late.from_core()

    def back_out(b):
        gy[b] = small[b, 5:6, :] * (nn(gbr[...], wout[b]) + nn(ghid[...], r.odn[b]))

    loop(BLOCKS, back_out)
    for k in range(2, tp_size):
        s_chain.step(tp == k)

    ssq, crs = r.ssq, r.crs
    ssq[...] = jnp.zeros_like(ssq)
    crs[...] = jnp.zeros_like(crs)

    def gated(b, c):
        full = y[b, rows(c), :] + r.skips[b, 8:9, :] * xs[b, rows(c), :]
        return full, full * gate[b, rows(c), :]

    def carried(b):
        state = r.s_in[b].astype(f32)
        for c in range(chunks):
            added = st[c, b]
            st[c, b] = state
            grown = nn(cb[rows(c), :], state.astype(bf16))
            y[b, rows(c), :] = y[b, rows(c), :] + nn(ech[rows(c), :], expand[b]) * grown
            state = r.et[b, c : c + 1, :] * state + added
            _, act = gated(b, c)
            ssq[rows(c), :] = ssq[rows(c), :] + thirds(act * act)
            crs[rows(c), :] = crs[rows(c), :] + thirds(act * gy[b, rows(c), :])
        st[chunks, b] = state

    loop(BLOCKS, carried)
    inner = BLOCKS * WIDE

    def settle(c):
        inv = lax.rsqrt(jnp.sum(ssq[rows(c), :], axis=1, keepdims=True) / inner + EPSILON)
        cross = jnp.sum(crs[rows(c), :], axis=1, keepdims=True) / inner
        ssq[rows(c), :] = jnp.broadcast_to(inv, (CHUNK, 128))
        crs[rows(c), :] = jnp.broadcast_to(inv * inv * inv * cross, (CHUNK, 128))

    loop(chunks, settle)

    acc, nout, hout, hout_t = r.acc, r.nout, r.hout, r.hout_t

    def out_block(b):
        def part(c):
            full, act = gated(b, c)
            inv, slope = ssq[rows(c), 0:1], crs[rows(c), 0:1]
            nout[rows(c), :] = (act * inv * small[b, 5:6, :]).astype(bf16)
            g_gated = inv * gy[b, rows(c), :] - act * slope
            g_y = g_gated * gate[b, rows(c), :]
            gy[b, rows(c), :] = g_y
            gzx[b, rows(c), :WIDE] = (g_gated * full * spz[b, rows(c), :].astype(f32)).astype(bf16)
            rt[c, b] = nn(ct[c], (nn(ech[rows(c), :], expand[b]) * g_y).astype(bf16))

        loop(chunks, part)
        et = r.et[b]
        total = rt[chunks - 1, b]
        for c in range(chunks - 2, -1, -1):
            total = total * et[c : c + 1] + rt[c, b]
        r.fresh[b] = total
        r.odg[b] = nn(r.ghid_t[...], nout[...])
        part_b = nt(nout[...], wout[b])
        part_h = nt(nout[...], r.odn[b])
        part_t = nt(r.odn[b], nout[...])

        @pl.when(b == 0)
        def _():
            acc[...] = part_b
            hout[...] = part_h
            hout_t[...] = part_t

        @pl.when(b > 0)
        def _():
            acc[...] = acc[...] + part_b
            hout[...] = hout[...] + part_h
            hout_t[...] = hout_t[...] + part_t

    loop(BLOCKS, out_block)
    r_chain.begin()

    def write_out(c):
        branch = acc[rows(c), :] + nn(hout[rows(c), :].astype(bf16), r.oup[...])
        u = ext[rows(c, HALO), :].astype(f32)
        r.out_rows[rows(c), :] = (u + valid(c) * branch).astype(bf16)

    loop(chunks, write_out)
    oug = nn(hout_t[...].astype(bf16), gbr[...])
    r_chain.step(r_chain.place == 1)
    if direct:
        write_back = pltpu.make_async_copy(r.out_rows, r.out, r.own_sem.at[5])
        write_back.start()
        rest = Sums(r, dp, tp, dp_size, tp_size, 1)
        for k in range(2):
            pair = jnp.concatenate([r.odg[2 * k], r.odg[2 * k + 1]], axis=1)
            r.sum_out[1, k] = pair.astype(bf16)
        r.sum_out[1, 2] = oug.astype(bf16)
        r.sum_out[1, 3] = jnp.zeros((16, gbr.shape[1]), bf16)
        rest.start()
    else:
        r.oug[...] = oug

    dsc = r.dsc
    dsc[...] = jnp.zeros_like(dsc)

    def inside_back(b):
        turn_heads(b)

        def part(c):
            total = dsc[c]
            for i in range(HEADS_B // 2):
                lanes, mixing, weights, split = pair_terms(b, c, i)
                g = gy[b, rows(c), lanes].astype(bf16)
                both = nt(g, split) * mixing
                total = total + both[:, :CHUNK] + both[:, CHUNK:]
                back = tn(weights, g)
                xp[b, rows(c), lanes] = jnp.where(half, back[:CHUNK], back[CHUNK:])
            dsc[c] = total

        loop(chunks, part)
        r_chain.step(jnp.logical_and(b == 2, r_chain.place == 2))
        if direct:

            @pl.when(b == 1)
            def _():
                rest.middle()

    loop(BLOCKS, inside_back)
    for k in range(3, tp_size):
        r_chain.step(r_chain.place == k)
    if direct:
        rest.gathered()

    h1, h2, db, dc = r.h1, r.h2, r.db, r.dc
    for ref in (h1, h2, db, dc):
        ref[...] = jnp.zeros_like(ref)
    hs = r.hs
    hs[...] = jnp.zeros_like(hs)

    def head_sum(v, b):
        parts = two_part(v)
        sel = expand[b, :CHUNK, :]
        return nt(parts[:, :WIDE], sel) + nt(parts[:, WIDE:], sel)

    def carried_back(b, part):
        for c in part:
            state = (r.r_in[b].astype(f32) if c == chunks - 1 else r.fresh[b])
            low = state.astype(bf16)
            meet = jnp.broadcast_to(jnp.sum(state * st[c + 1, b], axis=0, keepdims=True), (8, WIDE))
            hs[c] = hs[c] + head_sum(meet, b)
            tail = nn(tlh[rows(c), :], expand[b])
            grow = nn(ech[rows(c), :], expand[b])
            dt = nn(dth[rows(c), :], expand[b])
            x, g = xs[b, rows(c), :], gy[b, rows(c), :]
            back = xp[b, rows(c), :] + tail * nn(bb[rows(c), :], low)
            xdt = x * dt
            h1[rows(c), :] = h1[rows(c), :] + head_sum(g * y[b, rows(c), :] - xdt * back, b)
            h2[rows(c), :] = h2[rows(c), :] + head_sum(x * back, b)
            dc[rows(c), :] = dc[rows(c), :] + nt((grow * g).astype(bf16), st[c, b].astype(bf16))
            db[rows(c), :] = db[rows(c), :] + nt((tail * xdt).astype(bf16), low)
            px[b, rows(c), :] = (dt * back + r.skips[b, 8:9, :] * g) * spx[b, rows(c), :].astype(f32)
            r.fresh[b] = r.et[b, c : c + 1, :] * state + rt[c, b]

    up_tri = jnp.where(
        lax.broadcasted_iota(jnp.int32, (CHUNK, CHUNK), 0) <= lax.broadcasted_iota(jnp.int32, (CHUNK, CHUNK), 1),
        1.0,
        0.0,
    ).astype(f32)
    gdt = r.gdt

    def finish_bc(c):
        low = jnp.where(low_tri, dsc[c], 0.0).astype(bf16)
        d_c = dc[rows(c), :] + nn(low, bb[rows(c), :])
        d_b = db[rows(c), :] + tn(low, cb[rows(c), :])
        u = ub[rows(c), :]
        s = sigmoid(u)
        pb[rows(c), :] = jnp.concatenate([d_b, d_c], axis=1) * (s + u * s * (1.0 - s))
        da = jnp.dot(up_tri, h1[rows(c), :], precision=HIGHEST, preferred_element_type=f32) + hs[c, 0:1, :]
        gdt[rows(c), :] = ((h2[rows(c), :] + decay * da) * sigmoid(pd[rows(c), :])).astype(bf16)

    def edges():
        return [
            remote(r.ex_out, r.ex_in, r.e_ss.at[0], r.e_rs.at[0], (dp, before)),
            remote(r.eb_out, r.eb_in, r.e_ss.at[1], r.e_rs.at[1], (dp, before)),
        ]

    def send_edges():
        @pl.when(jnp.logical_not(at_first))
        def _():
            for b in range(BLOCKS):
                r.ex_out[b] = px[b, 0:8, :]
            r.eb_out[...] = pb[0:8, :]
            for copy in edges():
                copy.start()

    def take_edges():
        @pl.when(jnp.logical_not(at_last))
        def _():
            for copy in edges():
                copy.wait_recv()
            for b in range(BLOCKS):
                px[b, rows_n : rows_n + 8, :] = r.ex_in[b]
            pb[rows_n : rows_n + 8, :] = r.eb_in[...]

        @pl.when(at_last)
        def _():
            for b in range(BLOCKS):
                px[b, rows_n : rows_n + 8, :] = jnp.zeros((8, WIDE), f32)
            pb[rows_n : rows_n + 8, :] = jnp.zeros((8, 256), f32)

    def conv_back(window, kernel_row):
        size = window.shape[0] - 8
        total = kernel_row(3) * window[:size]
        for j in range(3):
            shifted = pltpu.roll(window, window.shape[0] - (3 - j), 0)
            total = total + kernel_row(j) * shifted[:size]
        return total

    if direct:
        returns = Returns(r, dp, tp, dp_size)

    def finish_rows(at, size):
        here = slice(at, at + size)
        gbc = conv_back(pb[at : at + size + 8, :], lambda j: bc_kernel[j : j + 1, :]).astype(bf16)
        acc[here, :] = nt(gbc, r.wbc[...]) + nt(gdt[here, :], r.wdt[...])
        hout[here, :] = jnp.zeros((size, 16), f32)

        def in_block(b):
            g = conv_back(px[b, at : at + size + 8, :], lambda j: small[b, j : j + 1, :]).astype(bf16)
            gzx[b, here, WIDE:] = g
            both = gzx[b, here, :]
            acc[here, :] = acc[here, :] + nt(both, zx[b])
            hout[here, :] = hout[here, :] + nt(both, up[b])

        loop(BLOCKS, in_block)
        g = acc[here, :] + nn(hout[here, :].astype(bf16), r.idn[...])
        u = ext[at + HALO : at + HALO + size, :].astype(f32)
        inv = lax.rsqrt(jnp.mean(u * u, axis=1, keepdims=True) + EPSILON)
        v = r.gain[...].astype(f32)[None] * g
        cross = jnp.mean(v * u, axis=1, keepdims=True)
        r.tg[here, :] = (cot[here, :].astype(f32) + inv * v - u * (inv * inv * inv * cross)).astype(bf16)
        if direct:
            for d in range(at // returns.block, (at + size) // returns.block):
                returns.send(d)

    upper = range(chunks - 1, chunks // 2 - 1, -1)
    lower = range(chunks // 2 - 1, -1, -1)
    loop(BLOCKS, lambda b: carried_back(b, upper))
    for c in upper:
        finish_bc(c)
    middle = rows_n // 2
    finish_rows(middle, middle - 64)
    if direct:
        rest.pass_on()
    loop(BLOCKS, lambda b: carried_back(b, lower))
    for c in lower:
        finish_bc(c)
    send_edges()
    finish_rows(0, middle)
    take_edges()
    finish_rows(rows_n - 64, 64)

    hid_t = nt(r.idn[...], nrm[HALO:, :]).astype(bf16)
    ghin_t = hout_t
    ghin_t[...] = jnp.zeros_like(ghin_t)

    def adapter_grads(b):
        g = gzx[b]
        ghin_t[...] = ghin_t[...] + nt(up[b], g)
        iug = nn(hid_t, g)
        if direct:
            r.sum_out[0, b] = iug.astype(bf16)
        else:
            r.iug[b] = iug

    loop(BLOCKS, adapter_grads)
    idg = nn(ghin_t[...].astype(bf16), nrm[HALO:, :])
    if direct:
        ups = Sums(r, dp, tp, dp_size, tp_size, 0)
        ups.start()
        ends = Toward(
            tp,
            tp_size,
            lambda t: (dp, t),
            lambda t: r.end_out,
            lambda t: r.end_in.at[t],
            r.ge_ss,
            r.ge_rs,
        )
        r.end_out[...] = idg.astype(bf16)
        ends.start()
        r.end_in[tp] = r.end_out[...]
        ups.middle()
        ends.wait()
        total = r.end_in[0].astype(f32)
        for t in range(1, BLOCKS):
            total = total + r.end_in[t].astype(f32)
        r.end_all[...] = total.astype(bf16)
        spread = Toward(
            dp,
            dp_size,
            lambda d: (d, tp),
            lambda d: r.end_all,
            lambda d: r.all_end.at[d],
            r.gf_ss,
            r.gf_rs,
        )
        spread.start()
        own_end = pltpu.make_async_copy(r.end_all, r.all_end.at[dp], r.own_sem.at[6])
        own_end.start()
        ups.gathered()
        spread.wait()
        own_end.wait()
        returns.finish()
        rest.finish()
        ups.finish()
        ends.finish()
        spread.finish()
        write_back.wait()
        end_front()
    else:
        r.idg[...] = idg
    s_chain.end()
    r_chain.end()

    @pl.when(jnp.logical_not(at_first))
    def _():
        for copy in edges():
            copy.wait_send()


def settle_kernel(dealt, adapters, out, tg, ups, rest, ends, o_out, o_tok, o_idg, o_iug, o_odg, o_oug, *scratch):
    v_out, v_tg, v_ups, v_rest, v_ends, s_idg, s_iug, s_odg, s_oug, sems = scratch
    count = dealt.shape[0]
    loads = [
        pltpu.make_async_copy(src, dst, sems.at[i])
        for i, (src, dst) in enumerate(((out, v_out), (tg, v_tg), (ups, v_ups), (rest, v_rest), (ends, v_ends)))
    ]
    for copy in loads:
        copy.start()
    for ref in (s_idg, s_iug, s_odg, s_oug):
        ref[...] = jnp.zeros_like(ref)
    loads[0].wait()
    stores = [pltpu.make_async_copy(v_out, o_out, sems.at[5])]
    stores[0].start()
    loads[1].wait()
    for s in range(count):
        stores.append(pltpu.make_async_copy(v_tg.at[dealt[s]], o_tok.at[s], sems.at[6 + s]))
        stores[-1].start()
    for copy in loads[2:]:
        copy.wait()
    half = 2 * WIDE
    for s in range(count):
        k, g = adapters[s], dealt[s]
        s_idg[k] = s_idg[k] + v_ends[g].astype(f32)
        for i in range(2):
            s_iug[k, :, i, :] = s_iug[k, :, i, :] + v_ups[g, :, i * WIDE : (i + 1) * WIDE].astype(f32)
            s_odg[k, :, i * half : (i + 1) * half] = s_odg[k, :, i * half : (i + 1) * half] + v_rest[i, g].astype(f32)
        s_oug[k] = s_oug[k] + v_rest[2, g].astype(f32)
    for i, (src, dst) in enumerate(((s_idg, o_idg), (s_iug, o_iug), (s_odg, o_odg), (s_oug, o_oug))):
        stores.append(pltpu.make_async_copy(src, dst, sems.at[6 + count + i]))
        stores[-1].start()
    for copy in stores:
        copy.wait()


def settle_call(dealt, adapters, res):
    n, block, d = res.tg_in.shape
    smem, any_space = pl.BlockSpec(memory_space=pltpu.SMEM), pl.BlockSpec(memory_space=pl.ANY)
    grads = [
        jax.ShapeDtypeStruct((ADAPTERS, 16, d), f32),
        jax.ShapeDtypeStruct((ADAPTERS, 16, 2, WIDE), f32),
        jax.ShapeDtypeStruct((ADAPTERS, 16, BLOCKS * WIDE), f32),
        jax.ShapeDtypeStruct((ADAPTERS, 16, d), f32),
    ]
    gathered = (res.out, res.tg_in, res.all_up, res.all_rest, res.all_end)
    return pl.pallas_call(
        settle_kernel,
        out_shape=[
            jax.ShapeDtypeStruct(res.out.shape, bf16),
            jax.ShapeDtypeStruct((n, block, d), bf16),
        ]
        + grads,
        in_specs=[smem] * 2 + [any_space] * 5,
        out_specs=[any_space] * 6,
        scratch_shapes=[pltpu.VMEM(v.shape, v.dtype) for v in gathered]
        + [pltpu.VMEM(v.shape, v.dtype) for v in grads]
        + [pltpu.SemaphoreType.DMA((10 + n,))],
    )(dealt, adapters, *gathered)


def mixer_call(direct, scalars, arrays):
    rows_n = arrays["cot"].shape[0]
    chunks = rows_n // CHUNK
    d = arrays["cot"].shape[1]
    outs = dict(
        out=((rows_n, d), bf16),
        tg=((rows_n, d), bf16),
        idg=((16, d), f32),
        iug=((BLOCKS, 16, 2 * WIDE), f32),
        odg=((BLOCKS, 16, WIDE), f32),
        oug=((16, d), f32),)
    wide = (BLOCKS, rows_n, WIDE)
    state = (BLOCKS, 128, WIDE)
    scratch = dict(
        idn=((16, d), bf16),
        oup=((16, d), bf16),
        odn=((BLOCKS, 16, WIDE), bf16),
        expand=((BLOCKS, 256, WIDE), bf16),
        skip=((16, 256), bf16),
        decay=((8, 128), f32),
        ghid_t=((16, rows_n), bf16),
        skips=((BLOCKS, 16, WIDE), f32),
        nrm=((rows_n + HALO, d), bf16),
        hid=((rows_n + HALO, 16), bf16),
        gate=(wide, f32),
        spz=(wide, bf16),
        px=((BLOCKS, rows_n + HALO, WIDE), f32),
        xs=(wide, f32),
        spx=(wide, bf16),
        xd=(wide, bf16),
        pb=((rows_n + HALO, 256), f32),
        pd=((rows_n, 128), f32),
        dth=((rows_n, 256), bf16),
        ech=((rows_n, 256), bf16),
        tlh=((rows_n, 256), bf16),
        eth=((16, 256), bf16),
        et=((BLOCKS, 16, WIDE), f32),
        cu=((rows_n, 128), f32),
        cub=((rows_n, 128), f32),
        cut=((chunks, 128, 128), f32),
        tot=((16, 128), f32),
        ub=((rows_n, 256), f32),
        bb=((rows_n, 128), bf16),
        cb=((rows_n, 128), bf16),
        bt=((chunks, 128, 128), bf16),
        ct=((chunks, 128, 128), bf16),
        sc=((chunks, 128, 128), f32),
        st=((chunks + 1,) + state, f32),
        rt=((chunks,) + state, f32),
        fresh=(state, f32),
        s_in=(state, bf16),
        s_out=(state, bf16),
        r_in=(state, bf16),
        r_out=(state, bf16),
        y=(wide, f32),
        gy=(wide, f32),
        gzx=((BLOCKS, rows_n, 2 * WIDE), bf16),
        gbr=((rows_n, d), bf16),
        ghid=((rows_n, 16), bf16),
        ssq=((rows_n, 128), f32),
        crs=((rows_n, 128), f32),
        acc=((rows_n, d), f32),
        nout=((rows_n, WIDE), bf16),
        hout=((rows_n, 16), f32),
        hout_t=((16, rows_n), f32),
        dsc=((chunks, 128, 128), f32),
        h1=((rows_n, 128), f32),
        h2=((rows_n, 128), f32),
        db=((rows_n, 128), f32),
        dc=((rows_n, 128), f32),
        hs=((chunks, 8, 128), f32),
        gdt=((rows_n, 128), bf16),
        ex_out=((BLOCKS, 8, WIDE), f32),
        ex_in=((BLOCKS, 8, WIDE), f32),
        eb_out=((8, 256), f32),
        eb_in=((8, 256), f32),)
    sems = dict(s_ss=(BLOCKS,), s_rs=(BLOCKS,), r_ss=(BLOCKS,), r_rs=(BLOCKS,), e_ss=(2,), e_rs=(2,))
    if direct:
        n, block = arrays["tokens"].shape[:2]
        scratch.update(iug=outs["iug"], odg=outs["odg"])
        outs = dict(
            out=((rows_n, d), bf16),
            tg_in=((n, block, d), bf16),
            all_up=((n, 16, d), bf16),
            all_rest=((BLOCKS, n, 16, d), bf16),
            all_end=((n, 16, d), bf16),
        )
        scratch.update(
            out_rows=((rows_n, d), bf16),
            tok_out=((n, block, d), bf16),
            ext=((rows_n + HALO, d), bf16),
            zx=((BLOCKS, d, 2 * WIDE), bf16),
            wout=((BLOCKS, d, WIDE), bf16),
            wbc=((d, 256), bf16),
            dts=((BLOCKS, n, 16, 128), bf16),
            wdt=((d, 128), bf16),
            up=((BLOCKS, 16, 2 * WIDE), bf16),
            small=((BLOCKS, 16, WIDE), f32),
            sum_out=((2, BLOCKS, 16, d), bf16),
            sum_in=((2, BLOCKS, 16, d), bf16),
            sum_all=((2, 16, d), bf16),
            end_out=((16, d), bf16),
            end_in=((BLOCKS, 16, d), bf16),
            end_all=((16, d), bf16),
        )
        for name in LOADED:
            scratch["v_" + name] = (arrays[name].shape, arrays[name].dtype)
        pairs = dict(zx=(6, n), wo=(6, n), bc=(3, n), tok=(n,), dt=(n,), d2=(BLOCKS,), up=(BLOCKS,), sm=(BLOCKS,))
        pairs.update(ha=(1,), tg=(n,), ga=(BLOCKS,), gb=(BLOCKS,), gc=(n,), gd=(n,), g3=(BLOCKS,))
        pairs.update(ge=(BLOCKS,), gf=(n,))
        for name, shape in pairs.items():
            sems[name + "_ss"] = shape
            sems[name + "_rs"] = (BLOCKS, n) if name in ("zx", "wo") else shape[-1:]
        sems.update(own_sem=(7,), load_sem=(len(LOADED),))
    names = list(scalars) + list(arrays) + list(outs) + list(scratch) + list(sems)
    smem = pl.BlockSpec(memory_space=pltpu.SMEM)
    vmem = pl.BlockSpec(memory_space=pl.ANY if direct else pltpu.VMEM)
    results = pl.pallas_call(
        partial(mixer_kernel, direct, names),
        out_shape=[jax.ShapeDtypeStruct(*v) for v in outs.values()],
        in_specs=[smem] * len(scalars) + [vmem] * len(arrays),
        out_specs=[vmem] * len(outs),
        scratch_shapes=[pltpu.VMEM(*v) for v in scratch.values()]
        + [pltpu.SemaphoreType.DMA(n) for n in sems.values()],
        compiler_params=pltpu.CompilerParams(
            collective_id=1, has_side_effects=True, vmem_limit_bytes=63 * 1024 * 1024
        ),
    )(*scalars.values(), *arrays.values())
    return SimpleNamespace(**dict(zip(outs, results)))


def pack_small(x_kernel, x_offset, out_gain, dt_bias, a_log, d_skip):
    def block(v):
        return v.reshape(-1, BLOCKS, v.shape[-1] // BLOCKS).transpose(1, 0, 2)

    def heads(v):
        return jnp.pad(block(v[None]), ((0, 0), (0, 0), (0, WIDE - HEADS_B)))

    parts = [
        block(x_kernel),
        block(x_offset[None]),
        block(out_gain.astype(f32)[None]),
        heads(dt_bias),
        heads(a_log),
        heads(d_skip),
        jnp.zeros((BLOCKS, 7, WIDE), f32),
    ]
    return jnp.concatenate(parts, axis=1)


def shards(
    tokens,
    cotangent,
    lengths,
    dealt_to,
    adapter_id,
    norm_gain,
    w_zx,
    w_dt,
    w_bc,
    x_kernel,
    x_offset,
    bc_kernel,
    bc_offset,
    dt_bias,
    a_log,
    d_skip,
    out_gain,
    w_out,
    inlet_down,
    inlet_up,
    outlet_down,
    outlet_up,
):
    d = tokens.shape[3]
    tp_size, dp_size = lax.axis_size("tensor"), lax.axis_size("dp")
    if tp_size == BLOCKS and dp_size % 2 == 0 and w_bc.shape[0] % 16 == 0 and tokens.shape[2] * 2 <= CHUNK:
        n, block = tokens.shape[0], tokens.shape[2]
        res = mixer_call(
            True,
            dict(lengths=lengths, dealt_to=dealt_to, adapter_id=adapter_id),
            dict(
                tokens=tokens.reshape(n, block, d),
                cot=cotangent.reshape(-1, d),
                gain=norm_gain,
                w_zx=w_zx,
                w_out=w_out.T,
                w_bc=w_bc,
                w_dt_in=w_dt.T,
                x_kernel=x_kernel,
                x_offset=x_offset,
                out_gain=out_gain,
                dt_bias=dt_bias,
                a_log=a_log,
                d_skip=d_skip,
                bc_kernel=bc_kernel,
                bc_offset=bc_offset,
                inlet_down=inlet_down.transpose(0, 2, 1),
                inlet_up=inlet_up,
                outlet_down=outlet_down.transpose(0, 2, 1),
                outlet_up=outlet_up,
            ),
        )
        out, tok, idg, iug, odg, oug = settle_call(dealt_to, adapter_id, res)
        return (
            out.reshape(1, -1, d),
            tok.reshape(tokens.shape),
            idg.transpose(0, 2, 1),
            iug,
            odg.transpose(0, 2, 1),
            oug,
        )
    group_id, place = lax.axis_index("dp"), lax.axis_index("tensor")
    seq_count = dealt_to.shape[0]
    slots = jnp.arange(seq_count, dtype=jnp.int32)
    seq_of = jnp.sum((dealt_to[None, :] == slots[:, None]).astype(jnp.int32) * slots[None, :], axis=1)
    own = jnp.take(seq_of, group_id)
    adapter = jnp.take(adapter_id, own)
    chosen = (jnp.arange(inlet_down.shape[0], dtype=jnp.int32) == adapter).astype(f32)

    picked = jnp.take(tokens, seq_of, axis=0)
    tok = lax.all_to_all(picked, "dp", split_axis=0, concat_axis=2, tiled=True).reshape(-1, d)
    rows_n = tok.shape[0]
    ends = lax.ppermute(tok[-HALO:], "tensor", [(i, i + 1) for i in range(tp_size - 1)])
    ext = jnp.concatenate([ends, tok], axis=0)

    def both(v, axis_dp, axis_tp):
        v = lax.all_gather(v, "dp", axis=axis_dp, tiled=True)
        return lax.all_gather(v, "tensor", axis=axis_tp, tiled=True)

    full_zx = both(w_zx, 0, 2)
    full_out = both(w_out, 1, 0)
    full_dt = both(w_dt, 0, 1)
    full_bc = lax.all_gather(w_bc, "dp", axis=0, tiled=True)
    zx = full_zx.reshape(d, 2, BLOCKS, WIDE).transpose(2, 0, 1, 3).reshape(BLOCKS, d, 2 * WIDE)
    wout = full_out.T.reshape(d, BLOCKS, WIDE).transpose(1, 0, 2)
    wdt = jnp.pad(full_dt.reshape(d, BLOCKS, HEADS_B), ((0, 0), (0, 0), (0, SLOT - HEADS_B))).reshape(d, BLOCKS * SLOT)
    wdt = jnp.pad(wdt, ((0, 0), (0, 128 - BLOCKS * SLOT)))

    def over_tp(v):
        return lax.all_gather(v, "tensor", axis=v.ndim - 1, tiled=True)

    small = pack_small(*(over_tp(v) for v in (x_kernel, x_offset, out_gain, dt_bias, a_log, d_skip)))
    up = over_tp(jnp.take(inlet_up, adapter, axis=0))
    up = up.reshape(16, 2, BLOCKS, WIDE).transpose(2, 0, 1, 3).reshape(BLOCKS, 16, 2 * WIDE)

    res = mixer_call(
        False,
        dict(lengths=lengths, dealt_to=dealt_to, adapter_id=adapter_id),
        dict(
            ext=ext,
            cot=cotangent.reshape(rows_n, d),
            gain=norm_gain,
            zx=zx,
            wout=wout,
            wbc=full_bc,
            wdt=wdt,
            small=small,
            up=up,
            bc_kernel=bc_kernel,
            bc_offset=bc_offset,
            inlet_down=inlet_down.transpose(0, 2, 1),
            outlet_down=outlet_down.transpose(0, 2, 1),
            outlet_up=outlet_up,
        ),
    )
    output = res.out.reshape(1, rows_n, d)
    returned = lax.all_to_all(res.tg.reshape(1, 1, rows_n, d), "dp", split_axis=2, concat_axis=0, tiled=True)
    token_grads = jnp.take(returned, dealt_to, axis=0)
    pick = chosen[:, None, None]
    odg = res.odg.transpose(1, 0, 2).reshape(16, BLOCKS * WIDE)
    idg, odg, oug = lax.psum((pick * res.idg[None], pick * odg[None], pick * res.oug[None]), ("dp", "tensor"))
    iug = res.iug.reshape(BLOCKS, 16, 2, WIDE).transpose(1, 2, 0, 3).reshape(16, 2, BLOCKS * WIDE)
    iug = lax.psum_scatter(iug, "tensor", scatter_dimension=2, tiled=True)
    iug = lax.psum(pick[..., None] * iug[None], "dp")
    return (output, token_grads, idg.transpose(0, 2, 1), iug, odg.transpose(0, 2, 1), oug)


def solution(mesh):
    in_specs = (
        P(None, "tensor", "dp", None),
        P("dp", "tensor", None),
        P(),
        P(),
        P(),
        P(),
        P("dp", None, "tensor"),
        P("dp", "tensor"),
        P("dp", None),
        P(None, "tensor"),
        P("tensor"),
        P(),
        P(),
        P("tensor"),
        P("tensor"),
        P("tensor"),
        P("tensor"),
        P("tensor", "dp"),
        P(),
        P(None, None, None, "tensor"),
        P(),
        P(),
    )
    out_specs = (
        P("dp", "tensor", None),
        P(None, "tensor", "dp", None),
        P(),
        P(None, None, None, "tensor"),
        P(),
        P(),
    )
    return jax.shard_map(shards, mesh=mesh, in_specs=in_specs, out_specs=out_specs, check_vma=False)
```

```python
from functools import partial
from types import SimpleNamespace

import jax
import jax.numpy as jnp
from jax import lax
from jax.experimental import pallas as pl
from jax.experimental.pallas import tpu as pltpu
from jax.sharding import PartitionSpec as P

EPSILON = 1e-05
LOG2E = 1.4426950408889634
HIGHEST = lax.Precision.HIGHEST
MESH = pl.DeviceIdType.MESH
f32, bf16 = jnp.float32, jnp.bfloat16

BLOCKS = 4
WIDE = 384
HEADS_B = 6
SLOT = 16
CHUNK = 128
HALO = 16
ADAPTERS = 8
TOK_AT = 2
LOADED = (
    "w_zx",
    "w_dt_in",
    "x_kernel",
    "x_offset",
    "out_gain",
    "dt_bias",
    "a_log",
    "d_skip",
    "inlet_up",
    "tokens",
    "cot",
    "gain",
    "bc_kernel",
    "bc_offset",
    "inlet_down",
    "outlet_up",
    "outlet_down",
)


def nn(a, b):
    return jnp.dot(a, b, preferred_element_type=f32)


def nt(a, b):
    return lax.dot_general(a, b, (((1,), (1,)), ((), ())), preferred_element_type=f32)


def tn(a, b):
    return lax.dot_general(a, b, (((0,), (0,)), ((), ())), preferred_element_type=f32)


def two_part(v):
    high = v.astype(bf16)
    return jnp.concatenate([high, (v - high.astype(f32)).astype(bf16)], axis=1)


def sigmoid(v):
    return 1.0 / (1.0 + jnp.exp(-v))


def thirds(v):
    return v[:, :128] + v[:, 128:256] + v[:, 256:384]


def loop(count, body, unroll=1):
    lax.fori_loop(0, count, lambda i, carry: (body(i), carry)[1], 0, unroll=unroll)


def remote(src, dst, ssem, rsem, peer):
    return pltpu.make_async_remote_copy(src, dst, ssem, rsem, device_id=peer, device_id_type=MESH)


class Spread:
    def __init__(self, buf, ssem, rsem, piece, dp, tp, dp_size, all_blocks):
        self.buf, self.ssem, self.rsem, self.piece = buf, ssem, rsem, piece
        self.dp, self.tp, self.nz, self.n = dp, tp, dp_size // 2, dp_size
        self.z, self.y = lax.div(dp, 2), lax.rem(dp, 2)
        self.all_blocks = all_blocks
        self.core = tp + 1 - 2 * lax.rem(tp, 2)
        self.far = lax.rem(tp + 2, 4)
        self.far_core = lax.rem(self.core + 2, 4)

    def at(self, t, d):
        rows = pl.ds(pl.multiple_of(d * self.piece, 16), self.piece)
        return self.buf.at[t, rows, :] if self.all_blocks else self.buf.at[rows, :]

    def copy(self, kind, t, d):
        peer = (
            (jnp.minimum(self.dp + 2, self.n - 1), self.tp),
            (jnp.maximum(self.dp - 2, 0), self.tp),
            (self.dp + 1 - 2 * self.y, self.tp),
            (self.dp, self.far),
            (self.dp, self.core),
            (self.dp, self.core),
        )[kind]
        rsem = self.rsem.at[t, d] if self.all_blocks else self.rsem.at[d]
        return remote(self.at(t, d), self.at(t, d), self.ssem.at[kind, d], rsem, peer)

    def wait(self, t, d):
        self.copy(2, t, d).wait_recv()

    def sideways(self, d):
        self.copy(2, self.tp, d).start()
        self.across(d)

    def across(self, d):
        if self.all_blocks:
            self.copy(3, self.tp, d).start()

    def column(self, t):
        peer = (self.dp, self.core)
        return remote(self.buf.at[t], self.buf.at[t], self.ssem.at[4, 0], self.rsem.at[t, 0], peer)

    def begin(self):
        @pl.when(self.z < self.nz - 1)
        def _():
            self.copy(0, self.tp, self.dp).start()

        @pl.when(self.z > 0)
        def _():
            self.copy(1, self.tp, self.dp).start()

        self.sideways(self.dp)

    def hop(self, k):
        low, high = self.dp - 2 * k, self.dp + 2 * k

        @pl.when(self.z >= k)
        def _():
            self.wait(self.tp, low)

            @pl.when(self.z < self.nz - 1)
            def _():
                self.copy(0, self.tp, low).start()

            self.sideways(low)

        @pl.when(self.z + k < self.nz)
        def _():
            self.wait(self.tp, high)

            @pl.when(self.z > 0)
            def _():
                self.copy(1, self.tp, high).start()

            self.sideways(high)

    def from_y(self, k):
        other = 1 - 2 * self.y
        low, high = self.dp + other - 2 * k, self.dp + other + 2 * k

        @pl.when(self.z >= k)
        def _():
            self.wait(self.tp, low)
            self.across(low)

        if k:

            @pl.when(self.z + k < self.nz)
            def _():
                self.wait(self.tp, high)
                self.across(high)

    def own_done(self):
        self.column(self.tp).start()

    def from_x(self):
        def forward(d):
            self.wait(self.far, d)
            self.copy(5, self.far, d).start()

        other = 1 - 2 * self.y
        for k in range(self.nz + 1):
            for shift, reach in ((0, k), (other, k - 1)):
                low, high = self.dp + shift - 2 * reach, self.dp + shift + 2 * reach
                if 0 <= reach < self.nz:

                    @pl.when(self.z >= reach)
                    def _(low=low):
                        forward(low)

                    if reach:

                        @pl.when(self.z + reach < self.nz)
                        def _(high=high):
                            forward(high)

    def from_core(self):
        self.column(self.core).wait_recv()
        self.from_far_core()

    def from_far_core(self):
        for k in range(self.n):
            self.wait(self.far_core, lax.rem(self.dp + k, self.n))

    def finish(self):
        for zz in range(self.nz):
            d = 2 * zz + self.y

            @pl.when(jnp.logical_and(self.z >= zz, self.z < self.nz - 1))
            def _():
                self.copy(0, self.tp, d).wait_send()

            @pl.when(jnp.logical_and(self.z <= zz, self.z > 0))
            def _():
                self.copy(1, self.tp, d).wait_send()

            self.copy(2, self.tp, d).wait_send()
        if self.all_blocks:
            for d in range(self.n):
                self.copy(3, self.tp, d).wait_send()
                self.copy(5, self.far, d).wait_send()
            self.column(self.tp).wait_send()


class Toward:
    def __init__(self, me, size, peer, src, dst, ssem, rsem):
        self.me, self.size, self.peer = me, size, peer
        self.src, self.dst, self.ssem, self.rsem = src, dst, ssem, rsem

    def copy(self, to, sender):
        return remote(self.src(to), self.dst(sender), self.ssem.at[to], self.rsem.at[sender], self.peer(to))

    def others(self):
        return [lax.rem(self.me + k, self.size) for k in range(1, self.size)]

    def start(self):
        for to in self.others():
            self.copy(to, self.me).start()

    def wait(self):
        for sender in self.others():
            self.copy(sender, sender).wait_recv()

    def finish(self):
        for to in self.others():
            self.copy(to, self.me).wait_send()


def front(r, dp, tp, dp_size, tp_size, load, scalars, work):
    block = r.tok_out.shape[1]
    rows_n = r.gbr.shape[0]
    piece = r.w_dt_in.shape[1]
    own_rows = pl.ds(pl.multiple_of(piece * dp, 16), piece)

    def place(d):
        return pl.ds(pl.multiple_of(HALO + block * d, 16), block)

    r.dts[tp, dp] = jnp.zeros_like(r.dts[tp, dp])
    r.small[tp] = jnp.zeros_like(r.small[tp])
    r.wdt[...] = jnp.zeros_like(r.wdt)
    own_out = pltpu.make_async_copy(r.w_out, r.wout.at[tp, own_rows, :], r.own_sem.at[0])
    own_bc = pltpu.make_async_copy(r.w_bc, r.wbc.at[own_rows, :], r.own_sem.at[1])
    own_out.start()
    own_bc.start()
    load.wait("w_zx")
    for k in range(2):
        r.zx[tp, own_rows, k * WIDE : (k + 1) * WIDE] = r.w_zx[:, k, :]
    own_bc.wait()
    work.greet()

    def to_dp(d):
        return (d, tp)

    def to_tp(t):
        return (dp, t)

    zx = Spread(r.zx, r.zx_ss, r.zx_rs, piece, dp, tp, dp_size, True)
    wout = Spread(r.wout, r.wo_ss, r.wo_rs, piece, dp, tp, dp_size, True)
    wbc = Spread(r.wbc, r.bc_ss, r.bc_rs, piece, dp, tp, dp_size, False)
    tok = Toward(dp, dp_size, to_dp, lambda d: r.tok_out.at[d], lambda d: r.ext.at[place(d), :], r.tok_ss, r.tok_rs)
    dts = Toward(dp, dp_size, to_dp, lambda d: r.dts.at[tp, dp], lambda d: r.dts.at[tp, d], r.dt_ss, r.dt_rs)
    dts2 = Toward(tp, tp_size, to_tp, lambda t: r.dts.at[tp], lambda t: r.dts.at[t], r.d2_ss, r.d2_rs)
    ups = Toward(tp, tp_size, to_tp, lambda t: r.up.at[tp], lambda t: r.up.at[t], r.up_ss, r.up_rs)
    smalls = Toward(tp, tp_size, to_tp, lambda t: r.small.at[tp], lambda t: r.small.at[t], r.sm_ss, r.sm_rs)

    zx.begin()
    wbc.begin()
    load.wait("w_dt_in", "x_kernel", "x_offset", "out_gain", "dt_bias", "a_log", "d_skip", "inlet_up")
    r.dts[tp, dp, 0:HEADS_B, 0:piece] = r.w_dt_in[...]
    r.small[tp, 0:4, :] = r.x_kernel[...]
    r.small[tp, 4, :] = r.x_offset[...]
    r.small[tp, 5, :] = r.out_gain[...].astype(f32)
    r.small[tp, 6, 0:HEADS_B] = r.dt_bias[...]
    r.small[tp, 7, 0:HEADS_B] = r.a_log[...]
    r.small[tp, 8, 0:HEADS_B] = r.d_skip[...]
    adapter = scalars.adapter()
    for k in range(2):
        r.up[tp, :, k * WIDE : (k + 1) * WIDE] = r.inlet_up[adapter, :, k, :]
    dts.start()
    ups.start()
    smalls.start()
    load.wait("tokens")
    for g in range(dp_size):
        r.tok_out[g] = r.tokens[scalars.seq_of(g)]
    r.ext[place(dp), :] = r.tok_out[dp]
    for k in range(1, zx.nz):
        zx.hop(k)
        zx.from_y(k - 1)
        if k == TOK_AT:
            tok.start()
        wbc.hop(k)
        wbc.from_y(k - 1)
    dts.wait()
    dts2.start()
    zx.from_y(zx.nz - 1)
    zx.own_done()
    wbc.from_y(zx.nz - 1)
    own_out.wait()
    work.early()
    dts2.wait()
    ups.wait()
    smalls.wait()
    for d in range(dp_size):
        lines = jnp.concatenate([r.dts[t, d].astype(f32) for t in range(BLOCKS)] * 2, axis=0)
        r.wdt[d * piece : (d + 1) * piece, :] = lines.T[:piece].astype(bf16)
    tok.wait()
    edge = remote(
        r.ext.at[rows_n : rows_n + HALO, :],
        r.ext.at[0:HALO, :],
        r.ha_ss.at[0],
        r.ha_rs.at[0],
        (dp, lax.rem(tp + 1, tp_size)),
    )

    @pl.when(tp < tp_size - 1)
    def _():
        edge.start()

    work.norm_own()

    @pl.when(tp > 0)
    def _():
        edge.wait_recv()

    @pl.when(tp == 0)
    def _():
        r.ext[0:HALO, :] = jnp.zeros((HALO, r.ext.shape[1]), bf16)

    work.norm_edge()
    work.project(tp)
    zx.from_x()
    wout.begin()
    zx.column(zx.core).wait_recv()
    work.project(zx.core)
    work.project_bc()
    work.project(zx.far)
    wout.hop(1)
    wout.from_y(0)
    zx.from_far_core()
    work.project(zx.far_core)

    def end():
        for part in (zx, wbc, wout, tok, dts, dts2, ups, smalls):
            part.finish()

        @pl.when(tp < tp_size - 1)
        def _():
            edge.wait_send()

    return wout, end


class Returns:
    def __init__(self, r, dp, tp, dp_size):
        self.r, self.dp, self.tp, self.n = r, dp, tp, dp_size
        self.block = r.tok_out.shape[1]

    def rows(self, d):
        return pl.ds(pl.multiple_of(self.block * d, 16), self.block)

    def copy(self, d, sender):
        r = self.r
        return remote(r.tg.at[self.rows(d), :], r.tg_in.at[sender], r.tg_ss.at[d], r.tg_rs.at[sender], (d, self.tp))

    def own(self):
        r = self.r
        return pltpu.make_async_copy(r.tg.at[self.rows(self.dp), :], r.tg_in.at[self.dp], r.own_sem.at[2])

    def send(self, d):
        @pl.when(d != self.dp)
        def _():
            self.copy(d, self.dp).start()

        @pl.when(d == self.dp)
        def _():
            self.own().start()

    def others(self):
        return [lax.rem(self.dp + k, self.n) for k in range(1, self.n)]

    def finish(self):
        self.own().wait()
        for d in self.others():
            self.copy(d, d).wait_recv()
        for d in self.others():
            self.copy(d, self.dp).wait_send()


class Sums:
    def __init__(self, r, dp, tp, dp_size, tp_size, part):
        self.r, self.dp, self.tp, self.part = r, dp, tp, part

        def to_tp(t):
            return (dp, t)

        def to_dp(d):
            return (d, tp)

        sems = ((r.ga_ss, r.ga_rs), (r.gb_ss, r.gb_rs))[part]
        sends = ((r.gc_ss, r.gc_rs), (r.gd_ss, r.gd_rs))[part]
        dst = (r.all_up, r.all_rest)[part]
        self.first = Toward(tp, tp_size, to_tp, lambda t: r.sum_out.at[part, t], lambda t: r.sum_in.at[part, t], *sems)
        self.second = Toward(
            dp,
            dp_size,
            to_dp,
            lambda d: r.sum_all.at[part],
            lambda d: dst.at[d] if part == 0 else dst.at[tp, d],
            *sends,
        )
        self.own = pltpu.make_async_copy(
            r.sum_all.at[part], dst.at[dp] if part == 0 else dst.at[tp, dp], r.own_sem.at[3 + part]
        )
        self.core = tp + 1 - 2 * lax.rem(tp, 2)
        self.far = lax.rem(tp + 2, 4)

    def start(self):
        self.first.start()

    def middle(self):
        r, part = self.r, self.part
        r.sum_in[part, self.tp] = r.sum_out[part, self.tp]
        self.first.wait()
        total = r.sum_in[part, 0].astype(f32)
        for t in range(1, BLOCKS):
            total = total + r.sum_in[part, t].astype(f32)
        r.sum_all[part] = total.astype(bf16)
        self.second.start()
        self.own.start()

    def hop(self, kind, t, peer):
        rest = self.r.all_rest.at[t]
        return remote(rest, rest, self.r.g3_ss.at[kind], self.r.g3_rs.at[t], (self.dp, peer))

    def gathered(self):
        self.second.wait()
        self.own.wait()
        if self.part:
            self.hop(0, self.tp, self.far).start()
            self.hop(1, self.tp, self.core).start()

    def pass_on(self):
        self.hop(0, self.far, self.far).wait_recv()
        self.hop(2, self.far, self.core).start()

    def finish(self):
        if self.part:
            self.hop(1, self.core, self.core).wait_recv()
            self.hop(2, lax.rem(self.core + 2, 4), self.core).wait_recv()
            for kind, t in ((0, self.tp), (1, self.tp), (2, self.far)):
                self.hop(kind, t, self.core).wait_send()
        self.first.finish()
        self.second.finish()


class Loads:
    def __init__(self, r, names):
        self.copies = {}
        for i, name in enumerate(names):
            src, dst = getattr(r, name), getattr(r, "v_" + name)
            self.copies[name] = pltpu.make_async_copy(src, dst, r.load_sem.at[i])
            setattr(r, name, dst)

    def start(self):
        for copy in self.copies.values():
            copy.start()

    def wait(self, *names):
        for name in names:
            self.copies[name].wait()


def mixer_kernel(direct, names, *refs):
    r = SimpleNamespace(**dict(zip(names, refs)))
    dp, tp = lax.axis_index("dp"), lax.axis_index("tensor")
    tp_size = lax.axis_size("tensor")
    lengths, dealt, adapters = r.lengths, r.dealt_to, r.adapter_id
    rows_n = r.cot.shape[0]
    chunks = rows_n // CHUNK
    after, before = lax.rem(tp + 1, tp_size), lax.rem(tp + tp_size - 1, tp_size)

    dp_size = lax.axis_size("dp")
    barrier = pltpu.get_barrier_semaphore()
    peers = [(dp, after), (dp, before)]
    if direct:
        peers = [(dp, lax.rem(tp + k, tp_size)) for k in range(1, tp_size)]
        peers += [(lax.rem(dp + k, dp_size), tp) for k in range(1, dp_size)]
    for peer in peers:
        pl.semaphore_signal(barrier, inc=1, device_id=peer, device_id_type=MESH)

    def greet():
        pl.semaphore_wait(barrier, len(peers))

    def seq_of(g):
        seq = jnp.int32(0)
        for s in range(dealt.shape[0]):
            seq = jnp.where(dealt[s] == g, s, seq)
        return seq

    own = seq_of(dp)
    adapter, length = adapters[own], lengths[own]
    if direct:
        r.tg = r.gbr
        load = Loads(r, LOADED)
        load.start()
    else:
        r.out_rows = r.out
        greet()

    ext, nrm, hid, zx, up = r.ext, r.nrm, r.hid, r.zx, r.up
    gate, spz, px, xs, spx, xd = r.gate, r.spz, r.px, r.xs, r.spx, r.xd
    expand, small, pb, pd = r.expand, r.small, r.pb, r.pd
    eth, cu, cut, tot = r.eth, r.cu, r.cut, r.tot
    ub, bb, cb, bt, ct, sc = r.ub, r.bb, r.cb, r.bt, r.ct, r.sc
    st, rt, y, gy, gzx, xp = r.st, r.rt, r.y, r.gy, r.gzx, r.px

    def rows(c, base=0, size=CHUNK):
        return pl.ds(pl.multiple_of(c * CHUNK + base, 16), size)

    def valid(c):
        at = tp * rows_n + c * CHUNK + lax.broadcasted_iota(jnp.int32, (CHUNK, 1), 0)
        return jnp.where(at < length, 1.0, 0.0).astype(f32)

    def fill_expand(b):
        head = jnp.bitwise_and(lax.broadcasted_iota(jnp.int32, (256, WIDE), 0), 127)
        lane = lax.broadcasted_iota(jnp.int32, (256, WIDE), 1)
        expand[b] = jnp.where(head == SLOT * b + lax.shift_right_logical(lane, 6), 1.0, 0.0).astype(bf16)

    def take_adapter():
        r.idn[...] = r.inlet_down[adapter]
        r.oup[...] = r.outlet_up[adapter]
        for b in range(BLOCKS):
            r.odn[b] = r.outlet_down[adapter, :, b * WIDE : (b + 1) * WIDE]

    cot, gbr, ghid, wout = r.cot, r.gbr, r.ghid, r.wout

    def mask_cot(c):
        gbr[rows(c), :] = (cot[rows(c), :].astype(f32) * valid(c)).astype(bf16)

    def early():
        if direct:
            load.wait("cot", "gain", "bc_kernel", "bc_offset", "inlet_down", "outlet_up", "outlet_down")
        take_adapter()
        loop(BLOCKS, fill_expand)
        loop(chunks, mask_cot)
        ghid[...] = nt(gbr[...], r.oup[...]).astype(bf16)

    def norm_rows(at, size):
        u = ext[pl.ds(at, size), :].astype(f32)
        inv = lax.rsqrt(jnp.mean(u * u, axis=1, keepdims=True) + EPSILON)
        nrm[pl.ds(at, size), :] = (u * inv * r.gain[...].astype(f32)[None]).astype(bf16)

    def norm_own():
        loop(chunks, lambda c: norm_rows(pl.multiple_of(c * CHUNK + HALO, 16), CHUNK))

    def norm_edge():
        norm_rows(0, HALO)
        hid[...] = nt(nrm[...], r.idn[...]).astype(bf16)

    def project(b):
        p = nn(nrm[...], zx[b]) + nn(hid[...], up[b])
        gate[b] = p[HALO:, :WIDE]
        px[b] = p[:, WIDE:]

    low_tri = lax.broadcasted_iota(jnp.int32, (CHUNK, CHUNK), 0) >= lax.broadcasted_iota(
        jnp.int32, (CHUNK, CHUNK), 1
    )

    def head_lanes():
        total = small[0, :, :128]
        for b in range(1, BLOCKS):
            total = total + pltpu.roll(small[b, :, :128], SLOT * b, 1)
        return total

    def steps(c):
        tri = jnp.where(low_tri, 1.0, 0.0).astype(f32)
        p = pd[rows(c), :]
        e = jnp.exp(-jnp.abs(p))
        log1p = jnp.where(e < 0.01, e * (1.0 - e * (0.5 - e * (1.0 / 3.0))), jnp.log(1.0 + e))
        dt = jnp.maximum(p, 0.0) + log1p
        rate = r.decay[0:1, :] * LOG2E
        cum = jnp.dot(tri, dt * rate, precision=HIGHEST, preferred_element_type=f32)
        total = cum[CHUNK - 1 : CHUNK]
        cu[rows(c), :] = cum
        cut[c] = cum.T
        tot[pl.ds(c, 1), :] = total
        r.rates[c, 0:CHUNK, :] = two_part(jnp.exp2(cum))
        r.rates[c, CHUNK : 2 * CHUNK, :] = two_part(dt)
        r.rates[c, 2 * CHUNK :, :] = two_part(jnp.exp2(total - cum))

    bc_kernel, bc_offset = r.bc_kernel, r.bc_offset

    def conv(window, kernel_row, offset):
        total = offset + kernel_row(3) * window[8:]
        for j in range(3):
            shifted = pltpu.roll(window, window.shape[0] - (5 + j), 0)
            total = total + kernel_row(j) * shifted[:CHUNK]
        return total

    def make_bc(c):
        window = pb[pl.ds(pl.multiple_of(c * CHUNK + 8, 8), CHUNK + 8), :]
        u = conv(window, lambda j: bc_kernel[j : j + 1, :], bc_offset[...][None])
        v = u * sigmoid(u)
        ub[rows(c), :] = u
        b_rows, c_rows = v[:, :128], v[:, 128:]
        bb[rows(c), :] = b_rows.astype(bf16)
        cb[rows(c), :] = c_rows.astype(bf16)
        bt[c] = b_rows.T.astype(bf16)
        ct[c] = c_rows.T.astype(bf16)
        sc[c] = jnp.where(low_tri, nt(c_rows.astype(bf16), b_rows.astype(bf16)), 0.0)

    def project_bc():
        head_rows = head_lanes()
        r.decay[...] = jnp.broadcast_to(-jnp.exp(head_rows[7:8]), (8, 128))
        r.skip[...] = two_part(head_rows)
        pb[...] = nn(nrm[...], r.wbc[...])
        pd[...] = nn(nrm[HALO:, :], r.wdt[...]) + head_rows[6:7]
        tot[...] = jnp.zeros_like(tot)
        loop(chunks, steps)
        tot[chunks : chunks + 1, :] = jnp.sum(tot[0:chunks, :], axis=0, keepdims=True)
        eth[...] = two_part(jnp.exp2(tot[...]))
        loop(chunks, make_bc)

    if direct:
        work = SimpleNamespace(
            greet=greet, early=early, norm_own=norm_own, norm_edge=norm_edge, project=project, project_bc=project_bc
        )
        scalars = SimpleNamespace(adapter=lambda: adapter, seq_of=seq_of)
        late, end_front = front(r, dp, tp, dp_size, tp_size, load, scalars, work)
    else:
        early()
        norm_own()
        norm_edge()
        loop(BLOCKS, project)
        project_bc()
    decay = r.decay[0:1, :]

    class Chain:
        def __init__(self, src, dst, ssem, rsem, to, place):
            self.src, self.dst, self.ssem, self.rsem, self.to, self.place = src, dst, ssem, rsem, to, place

        def copy(self, b):
            return remote(self.src.at[b], self.dst.at[b], self.ssem.at[b], self.rsem.at[b], (dp, self.to))

        def begin(self, b):
            @pl.when(self.place == 0)
            def _():
                self.src[b] = r.fresh[b].astype(bf16)
                self.copy(b).start()
                self.dst[b] = jnp.zeros_like(self.dst[b])

        def step(self, cond, b):
            @pl.when(cond)
            def _():
                self.copy(b).wait_recv()

                @pl.when(self.place < tp_size - 1)
                def _():
                    grown = self.dst[b].astype(f32) * r.et[b][chunks : chunks + 1]
                    self.src[b] = (grown + r.fresh[b]).astype(bf16)
                    self.copy(b).start()

        def within(self, b):
            self.begin(b)
            for place, lag in ((1, 1), (2, 3)):
                self.step(jnp.logical_and(self.place == place, b >= lag), jnp.maximum(b - lag, 0))

        def after_first(self):
            self.step(self.place == 1, BLOCKS - 1)

        def between(self, b):
            @pl.when(b == 2)
            def _():
                for k in range(BLOCKS - 3, BLOCKS):
                    self.step(self.place == 2, k)

        def rest(self):
            for place in range(3, tp_size):
                for b in range(BLOCKS):
                    self.step(self.place == place, b)

        def end(self):
            @pl.when(self.place < tp_size - 1)
            def _():
                for b in range(BLOCKS):
                    self.copy(b).wait_send()

    at_first, at_last = tp == 0, tp == tp_size - 1
    s_chain = Chain(r.s_out, r.s_in, r.s_ss, r.s_rs, after, tp)
    r_chain = Chain(r.r_out, r.r_in, r.r_ss, r.r_rs, before, tp_size - 1 - tp)

    def make_x(b):
        def part(c):
            window = px[b, pl.ds(pl.multiple_of(c * CHUNK + 8, 8), CHUNK + 8), :]
            u = conv(window, lambda j: small[b, j : j + 1, :], small[b, 4:5, :])
            s = sigmoid(u)
            x = u * s
            xs[b, rows(c), :] = x
            spx[b, rows(c), :] = (s + x * (1.0 - s)).astype(bf16)
            wide = nn(r.rates[c, CHUNK:, :], expand[b])
            xdt = x * wide[:CHUNK]
            xd[b, rows(c), :] = xdt.astype(bf16)
            st[c, b] = nn(bt[c], (xdt * wide[CHUNK:]).astype(bf16))
            z = gate[b, rows(c), :]
            s = sigmoid(z)
            g = z * s
            gate[b, rows(c), :] = g
            spz[b, rows(c), :] = (s + g * (1.0 - s)).astype(bf16)

        loop(chunks, part, chunks)
        et = nn(eth[...], expand[b])
        r.et[b] = et
        r.skips[b] = nn(r.skip[...], expand[b])
        total = st[0, b]
        for c in range(1, chunks):
            total = total * et[c : c + 1] + st[c, b]
        r.fresh[b] = total
        s_chain.within(b)
        if direct:

            @pl.when(b == 0)
            def _():
                late.hop(2)
                late.from_y(1)

            @pl.when(b == 1)
            def _():
                late.hop(3)
                late.from_y(2)

            @pl.when(b == 2)
            def _():
                late.from_y(3)
                late.own_done()

    loop(BLOCKS, make_x)
    s_chain.after_first()

    half = lax.broadcasted_iota(jnp.int32, (CHUNK, 128), 1) < 64

    def pair_terms(b, c, i):
        lanes = slice(128 * i, 128 * (i + 1))
        cum = r.cub[rows(c), :]
        cols = jnp.concatenate(
            [jnp.broadcast_to(cum[:, 2 * i + k : 2 * i + k + 1], (CHUNK, CHUNK)) for k in range(2)], axis=1
        )
        line = jnp.concatenate([cut[c, pl.ds(SLOT * b + 2 * i + k, 1), :] for k in range(2)], axis=1)
        mixing = jnp.exp2(jnp.minimum(cols - line, 0.0))
        scores = sc[c]
        weights = (mixing * jnp.concatenate([scores, scores], axis=1)).astype(bf16)
        pair = xd[b, rows(c), lanes]
        none = jnp.zeros_like(pair)
        split = jnp.concatenate([jnp.where(half, pair, none), jnp.where(half, none, pair)], axis=0)
        return lanes, mixing, weights, split

    def turn_heads(b):
        for c in range(chunks):
            r.cub[rows(c), :] = pltpu.roll(cu[rows(c), :], lax.rem(128 - SLOT * b, 128), 1)

    def inside(b):
        turn_heads(b)

        def part(c):
            for i in range(HEADS_B // 2):
                lanes, mixing, weights, split = pair_terms(b, c, i)
                y[b, rows(c), lanes] = nn(weights, split)

        loop(chunks, part, chunks)
        s_chain.between(b)

    loop(BLOCKS, inside)
    if direct:
        late.from_x()
    s_chain.rest()

    ssq, crs = r.ssq, r.crs
    ssq[...] = jnp.zeros_like(ssq)
    crs[...] = jnp.zeros_like(crs)

    def gated(b, c):
        full = y[b, rows(c), :] + r.skips[b, 8:9, :] * xs[b, rows(c), :]
        return full, full * gate[b, rows(c), :]

    def carried(b):
        state = r.s_in[b].astype(f32)
        for c in range(chunks):
            added = st[c, b]
            st[c, b] = state
            grown = nn(cb[rows(c), :], state.astype(bf16))
            y[b, rows(c), :] = y[b, rows(c), :] + nn(r.rates[c, 0:CHUNK, :], expand[b]) * grown
            state = r.et[b, c : c + 1, :] * state + added
            _, act = gated(b, c)
            ssq[rows(c), :] = ssq[rows(c), :] + thirds(act * act)
        st[chunks, b] = state

    loop(BLOCKS, carried)
    if direct:
        late.from_core()

    def back_out(b):
        back = small[b, 5:6, :] * (nn(gbr[...], wout[b]) + nn(ghid[...], r.odn[b]))
        gy[b] = back
        for c in range(chunks):
            _, act = gated(b, c)
            crs[rows(c), :] = crs[rows(c), :] + thirds(act * back[c * CHUNK : (c + 1) * CHUNK])

    loop(BLOCKS, back_out)
    inner = BLOCKS * WIDE

    def settle(c):
        inv = lax.rsqrt(jnp.sum(ssq[rows(c), :], axis=1, keepdims=True) / inner + EPSILON)
        cross = jnp.sum(crs[rows(c), :], axis=1, keepdims=True) / inner
        ssq[rows(c), :] = jnp.broadcast_to(inv, (CHUNK, 128))
        crs[rows(c), :] = jnp.broadcast_to(inv * inv * inv * cross, (CHUNK, 128))

    loop(chunks, settle)

    acc, nout, hout = r.acc, r.nout, r.hout

    def out_block(b):
        def part(c):
            full, act = gated(b, c)
            inv, slope = ssq[rows(c), 0:1], crs[rows(c), 0:1]
            nout[rows(c), :] = (act * inv * small[b, 5:6, :]).astype(bf16)
            g_gated = inv * gy[b, rows(c), :] - act * slope
            g_y = g_gated * gate[b, rows(c), :]
            gy[b, rows(c), :] = g_y
            gzx[b, rows(c), :WIDE] = (g_gated * full * spz[b, rows(c), :].astype(f32)).astype(bf16)
            rt[c, b] = nn(ct[c], (nn(r.rates[c, 0:CHUNK, :], expand[b]) * g_y).astype(bf16))

        loop(chunks, part, chunks)
        et = r.et[b]
        total = rt[chunks - 1, b]
        for c in range(chunks - 2, -1, -1):
            total = total * et[c : c + 1] + rt[c, b]
        r.fresh[b] = total
        r_chain.within(b)
        r.odg[b] = tn(ghid[...], nout[...])
        part_b = nt(nout[...], wout[b])
        part_h = nt(nout[...], r.odn[b])

        @pl.when(b == 0)
        def _():
            acc[...] = part_b
            hout[...] = part_h

        @pl.when(b > 0)
        def _():
            acc[...] = acc[...] + part_b
            hout[...] = hout[...] + part_h

    loop(BLOCKS, out_block)
    r_chain.after_first()

    def write_out(c):
        branch = acc[rows(c), :] + nn(hout[rows(c), :].astype(bf16), r.oup[...])
        u = ext[rows(c, HALO), :].astype(f32)
        r.out_rows[rows(c), :] = (u + valid(c) * branch).astype(bf16)

    loop(chunks, write_out)
    oug = tn(hout[...].astype(bf16), gbr[...])
    if direct:
        write_back = pltpu.make_async_copy(r.out_rows, r.out, r.own_sem.at[5])
        write_back.start()
        rest = Sums(r, dp, tp, dp_size, tp_size, 1)
        for k in range(2):
            pair = jnp.concatenate([r.odg[2 * k], r.odg[2 * k + 1]], axis=1)
            r.sum_out[1, k] = pair.astype(bf16)
        r.sum_out[1, 2] = oug.astype(bf16)
        r.sum_out[1, 3] = jnp.zeros((16, gbr.shape[1]), bf16)
        rest.start()
    else:
        r.oug[...] = oug

    dsc = r.dsc
    dsc[...] = jnp.zeros_like(dsc)

    def inside_back(b, part):
        for c in part:
            r.cub[rows(c), :] = pltpu.roll(cu[rows(c), :], lax.rem(128 - SLOT * b, 128), 1)
        for c in part:
            total = dsc[c]
            for i in range(HEADS_B // 2):
                lanes, mixing, weights, split = pair_terms(b, c, i)
                g = gy[b, rows(c), lanes].astype(bf16)
                both = nt(g, split) * mixing
                total = total + both[:, :CHUNK] + both[:, CHUNK:]
                back = tn(weights, g)
                xp[b, rows(c), lanes] = jnp.where(half, back[:CHUNK], back[CHUNK:])
            dsc[c] = total

    upper, lower = range(chunks // 2, chunks), range(chunks // 2)

    def first_back(b):
        inside_back(b, upper)
        r_chain.between(b)

    loop(BLOCKS, first_back)
    r_chain.rest()
    if direct:
        rest.middle()

    h1, h2, db, dc = r.h1, r.h2, r.db, r.dc
    for ref in (h1, h2, db, dc):
        ref[...] = jnp.zeros_like(ref)
    hs = r.hs
    hs[...] = jnp.zeros_like(hs)

    def head_sum(v, b):
        parts = two_part(v)
        sel = expand[b, :CHUNK, :]
        return nt(parts[:, :WIDE], sel) + nt(parts[:, WIDE:], sel)

    def states_back(b):
        state = r.r_in[b].astype(f32)
        for c in range(chunks - 1, -1, -1):
            added = rt[c, b]
            rt[c, b] = state
            state = r.et[b, c : c + 1, :] * state + added

    loop(BLOCKS, states_back)

    def carried_back(b, c):
        state = rt[c, b]
        low = state.astype(bf16)
        meet = jnp.broadcast_to(jnp.sum(state * st[c + 1, b], axis=0, keepdims=True), (8, WIDE))
        hs[c] = hs[c] + head_sum(meet, b)
        wide = nn(r.rates[c], expand[b])
        grow, dt, tail = wide[:CHUNK], wide[CHUNK : 2 * CHUNK], wide[2 * CHUNK :]
        x, g = xs[b, rows(c), :], gy[b, rows(c), :]
        back = xp[b, rows(c), :] + tail * nn(bb[rows(c), :], low)
        h1[rows(c), :] = h1[rows(c), :] + head_sum(g * y[b, rows(c), :], b)
        h2[rows(c), :] = h2[rows(c), :] + head_sum(x * back, b)
        dc[rows(c), :] = dc[rows(c), :] + nt((grow * g).astype(bf16), st[c, b].astype(bf16))
        db[rows(c), :] = db[rows(c), :] + nt((tail * x * dt).astype(bf16), low)
        px[b, rows(c), :] = (dt * back + r.skips[b, 8:9, :] * g) * spx[b, rows(c), :].astype(f32)

    up_tri = jnp.where(
        lax.broadcasted_iota(jnp.int32, (CHUNK, CHUNK), 0) <= lax.broadcasted_iota(jnp.int32, (CHUNK, CHUNK), 1),
        1.0,
        0.0,
    ).astype(f32)
    gdt = r.gdt

    def finish_bc(c):
        low = jnp.where(low_tri, dsc[c], 0.0).astype(bf16)
        d_c = dc[rows(c), :] + nn(low, bb[rows(c), :])
        d_b = db[rows(c), :] + tn(low, cb[rows(c), :])
        u = ub[rows(c), :]
        s = sigmoid(u)
        pb[rows(c), :] = jnp.concatenate([d_b, d_c], axis=1) * (s + u * s * (1.0 - s))
        dt = r.rates[c, CHUNK : 2 * CHUNK, :128].astype(f32) + r.rates[c, CHUNK : 2 * CHUNK, 128:].astype(f32)
        dcum = h1[rows(c), :] - dt * h2[rows(c), :]
        da = jnp.dot(up_tri, dcum, precision=HIGHEST, preferred_element_type=f32) + hs[c, 0:1, :]
        gdt[rows(c), :] = ((h2[rows(c), :] + decay * da) * sigmoid(pd[rows(c), :])).astype(bf16)

    def edges():
        return [
            remote(r.ex_out, r.ex_in, r.e_ss.at[0], r.e_rs.at[0], (dp, before)),
            remote(r.eb_out, r.eb_in, r.e_ss.at[1], r.e_rs.at[1], (dp, before)),
        ]

    def send_edges():
        @pl.when(jnp.logical_not(at_first))
        def _():
            for b in range(BLOCKS):
                r.ex_out[b] = px[b, 0:8, :]
            r.eb_out[...] = pb[0:8, :]
            for copy in edges():
                copy.start()

    def take_edges():
        @pl.when(jnp.logical_not(at_last))
        def _():
            for copy in edges():
                copy.wait_recv()
            for b in range(BLOCKS):
                px[b, rows_n : rows_n + 8, :] = r.ex_in[b]
            pb[rows_n : rows_n + 8, :] = r.eb_in[...]

        @pl.when(at_last)
        def _():
            for b in range(BLOCKS):
                px[b, rows_n : rows_n + 8, :] = jnp.zeros((8, WIDE), f32)
            pb[rows_n : rows_n + 8, :] = jnp.zeros((8, 256), f32)

    def conv_back(window, kernel_row):
        size = window.shape[0] - 8
        total = kernel_row(3) * window[:size]
        for j in range(3):
            shifted = pltpu.roll(window, window.shape[0] - (3 - j), 0)
            total = total + kernel_row(j) * shifted[:size]
        return total

    if direct:
        returns = Returns(r, dp, tp, dp_size)

    def conv_rows(at, size):
        for b in range(BLOCKS):
            window = px[b, at : at + size + 8, :]
            g = conv_back(window, lambda j: small[b, j : j + 1, :]).astype(bf16)
            gzx[b, at : at + size, WIDE:] = g
        window = pb[at : at + size + 8, :]
        r.gbc[at : at + size, :] = conv_back(window, lambda j: bc_kernel[j : j + 1, :]).astype(bf16)

    def hidden_rows(at, size):
        here = slice(at, at + size)
        for b in range(BLOCKS):
            part = nt(gzx[b, here, :], up[b])
            hout[here, :] = part if b == 0 else hout[here, :] + part

    def finish_rows(at, size, blocks=(), skip=0):
        here = slice(at, at + size)
        turned = nt(zx[0], gzx[0, here, :])
        for b in range(1, BLOCKS):
            turned = turned + nt(zx[b], gzx[b, here, :])
        turned = turned + nt(r.wbc[...], r.gbc[here, :])
        turned = turned + nt(r.wdt[...], gdt[here, :])
        kept = slice(at + skip, at + size)
        g = turned.T[skip:] + nn(hout[kept, :].astype(bf16), r.idn[...])
        u = ext[at + skip + HALO : at + HALO + size, :].astype(f32)
        inv = lax.rsqrt(jnp.mean(u * u, axis=1, keepdims=True) + EPSILON)
        v = r.gain[...].astype(f32)[None] * g
        cross = jnp.mean(v * u, axis=1, keepdims=True)
        r.tg[kept, :] = (cot[kept, :].astype(f32) + inv * v - u * (inv * inv * inv * cross)).astype(bf16)
        if direct:
            for d in blocks:
                returns.send(d)

    block = r.tok_out.shape[1] if direct else CHUNK // 2
    middle = rows_n // 2
    loop(BLOCKS, lambda b: [carried_back(b, c) for c in upper])
    for c in upper:
        finish_bc(c)
    conv_rows(middle, middle - block)
    hidden_rows(middle, middle - block)
    if direct:
        finish_rows(middle, middle, range(middle // block, rows_n // block - 1))
    per = CHUNK // block
    for c in reversed(lower):
        loop(BLOCKS, lambda b: inside_back(b, (c,)))
        if direct and c == lower[-1]:
            rest.gathered()
        loop(BLOCKS, lambda b: carried_back(b, c), BLOCKS)
        finish_bc(c)
        if c == 0:
            send_edges()
        conv_rows(c * CHUNK, CHUNK)
        hidden_rows(c * CHUNK, CHUNK)
        if direct and c == lower[-1]:
            finish_rows(c * CHUNK, CHUNK, range(c * per, (c + 1) * per))
            rest.pass_on()
    take_edges()
    conv_rows(rows_n - block, block)
    hidden_rows(rows_n - block, block)

    def adapter_grads(b):
        iug = tn(hid[HALO:, :], gzx[b])
        if direct:
            r.sum_out[0, b] = iug.astype(bf16)
        else:
            r.iug[b] = iug

    loop(BLOCKS, adapter_grads, BLOCKS)
    idg = tn(hout[...].astype(bf16), nrm[HALO:, :])
    if not direct:
        for half in range(2):
            finish_rows(half * middle, middle)
    if direct:
        ups = Sums(r, dp, tp, dp_size, tp_size, 0)
        ups.start()
        to_tp = lambda t: (dp, t)
        ends = Toward(tp, tp_size, to_tp, lambda t: r.end_out.at[t], lambda t: r.end_in.at[t], r.ge_ss, r.ge_rs)
        low = idg.astype(bf16)
        for t in range(3):
            r.end_out[t] = low[:, t * 256 : (t + 1) * 256]
        r.end_out[3] = jnp.zeros_like(r.end_out[3])
        ends.start()
        r.end_in[tp] = r.end_out[tp]
        finish_rows(0, CHUNK)
        ups.middle()
        ends.wait()
        total = r.end_in[0].astype(f32)
        for t in range(1, BLOCKS):
            total = total + r.end_in[t].astype(f32)
        r.end_all[...] = total.astype(bf16)
        spread = Toward(
            dp,
            dp_size,
            lambda d: (d, tp),
            lambda d: r.end_all,
            lambda d: r.all_end.at[tp, d],
            r.gf_ss,
            r.gf_rs,
        )
        spread.start()
        for d in range(per):
            returns.send(d)
        finish_rows(rows_n - CHUNK, CHUNK, [rows_n // block - 1], CHUNK - block)
        own_end = pltpu.make_async_copy(r.end_all, r.all_end.at[tp, dp], r.own_sem.at[6])
        own_end.start()
        spread.wait()
        own_end.wait()
        wide_end = Toward(tp, tp_size, to_tp, lambda t: r.all_end.at[tp], lambda t: r.all_end.at[t], r.gg_ss, r.gg_rs)
        wide_end.start()
        ups.gathered()
        returns.finish()
        rest.finish()
        ups.finish()
        ends.finish()
        spread.finish()
        wide_end.wait()
        wide_end.finish()
        write_back.wait()
        end_front()
    else:
        r.idg[...] = idg
    s_chain.end()
    r_chain.end()

    @pl.when(jnp.logical_not(at_first))
    def _():
        for copy in edges():
            copy.wait_send()


def settle_kernel(dealt, adapters, out, tg, ups, rest, ends, o_out, o_tok, o_idg, o_iug, o_odg, o_oug, *scratch):
    v_out, v_tg, v_ups, v_rest, v_ends, s_idg, s_iug, s_odg, s_oug, sems = scratch
    count = dealt.shape[0]
    loads = [
        pltpu.make_async_copy(src, dst, sems.at[i])
        for i, (src, dst) in enumerate(((out, v_out), (tg, v_tg), (ups, v_ups), (rest, v_rest), (ends, v_ends)))
    ]
    for copy in loads:
        copy.start()
    for ref in (s_idg, s_iug, s_odg, s_oug):
        ref[...] = jnp.zeros_like(ref)
    loads[0].wait()
    stores = [pltpu.make_async_copy(v_out, o_out, sems.at[5])]
    stores[0].start()
    loads[1].wait()
    for s in range(count):
        stores.append(pltpu.make_async_copy(v_tg.at[dealt[s]], o_tok.at[s], sems.at[6 + s]))
        stores[-1].start()
    for copy in loads[2:]:
        copy.wait()
    half = 2 * WIDE
    for s in range(count):
        k, g = adapters[s], dealt[s]
        for i in range(3):
            lanes = slice(256 * i, 256 * (i + 1))
            s_idg[k, :, lanes] = s_idg[k, :, lanes] + v_ends[i, g].astype(f32)
        for i in range(2):
            s_iug[k, :, i, :] = s_iug[k, :, i, :] + v_ups[g, :, i * WIDE : (i + 1) * WIDE].astype(f32)
            s_odg[k, :, i * half : (i + 1) * half] = s_odg[k, :, i * half : (i + 1) * half] + v_rest[i, g].astype(f32)
        s_oug[k] = s_oug[k] + v_rest[2, g].astype(f32)
    for i, (src, dst) in enumerate(((s_idg, o_idg), (s_iug, o_iug), (s_odg, o_odg), (s_oug, o_oug))):
        stores.append(pltpu.make_async_copy(src, dst, sems.at[6 + count + i]))
        stores[-1].start()
    for copy in stores:
        copy.wait()


def settle_call(dealt, adapters, res):
    n, block, d = res.tg_in.shape
    smem, any_space = pl.BlockSpec(memory_space=pltpu.SMEM), pl.BlockSpec(memory_space=pl.ANY)
    grads = [
        jax.ShapeDtypeStruct((ADAPTERS, 16, d), f32),
        jax.ShapeDtypeStruct((ADAPTERS, 16, 2, WIDE), f32),
        jax.ShapeDtypeStruct((ADAPTERS, 16, BLOCKS * WIDE), f32),
        jax.ShapeDtypeStruct((ADAPTERS, 16, d), f32),
    ]
    gathered = (res.out, res.tg_in, res.all_up, res.all_rest, res.all_end)
    return pl.pallas_call(
        settle_kernel,
        out_shape=[
            jax.ShapeDtypeStruct(res.out.shape, bf16),
            jax.ShapeDtypeStruct((n, block, d), bf16),
        ]
        + grads,
        in_specs=[smem] * 2 + [any_space] * 5,
        out_specs=[any_space] * 6,
        scratch_shapes=[pltpu.VMEM(v.shape, v.dtype) for v in gathered]
        + [pltpu.VMEM(v.shape, v.dtype) for v in grads]
        + [pltpu.SemaphoreType.DMA((10 + n,))],
    )(dealt, adapters, *gathered)


def mixer_call(direct, scalars, arrays):
    rows_n = arrays["cot"].shape[0]
    chunks = rows_n // CHUNK
    d = arrays["cot"].shape[1]
    outs = dict(
        out=((rows_n, d), bf16),
        tg=((rows_n, d), bf16),
        idg=((16, d), f32),
        iug=((BLOCKS, 16, 2 * WIDE), f32),
        odg=((BLOCKS, 16, WIDE), f32),
        oug=((16, d), f32),)
    wide = (BLOCKS, rows_n, WIDE)
    state = (BLOCKS, 128, WIDE)
    scratch = dict(
        idn=((16, d), bf16),
        oup=((16, d), bf16),
        odn=((BLOCKS, 16, WIDE), bf16),
        expand=((BLOCKS, 256, WIDE), bf16),
        skip=((16, 256), bf16),
        decay=((8, 128), f32),
        skips=((BLOCKS, 16, WIDE), f32),
        nrm=((rows_n + HALO, d), bf16),
        hid=((rows_n + HALO, 16), bf16),
        gate=(wide, f32),
        spz=(wide, bf16),
        px=((BLOCKS, rows_n + HALO, WIDE), f32),
        xs=(wide, f32),
        spx=(wide, bf16),
        xd=(wide, bf16),
        pb=((rows_n + HALO, 256), f32),
        pd=((rows_n, 128), f32),
        rates=((chunks, 3 * CHUNK, 256), bf16),
        eth=((16, 256), bf16),
        et=((BLOCKS, 16, WIDE), f32),
        cu=((rows_n, 128), f32),
        cub=((rows_n, 128), f32),
        cut=((chunks, 128, 128), f32),
        tot=((16, 128), f32),
        ub=((rows_n, 256), f32),
        bb=((rows_n, 128), bf16),
        cb=((rows_n, 128), bf16),
        bt=((chunks, 128, 128), bf16),
        ct=((chunks, 128, 128), bf16),
        sc=((chunks, 128, 128), f32),
        st=((chunks + 1,) + state, f32),
        rt=((chunks,) + state, f32),
        fresh=(state, f32),
        s_in=(state, bf16),
        s_out=(state, bf16),
        r_in=(state, bf16),
        r_out=(state, bf16),
        y=(wide, f32),
        gy=(wide, f32),
        gzx=((BLOCKS, rows_n, 2 * WIDE), bf16),
        gbr=((rows_n, d), bf16),
        ghid=((rows_n, 16), bf16),
        ssq=((rows_n, 128), f32),
        crs=((rows_n, 128), f32),
        acc=((rows_n, d), f32),
        nout=((rows_n, WIDE), bf16),
        hout=((rows_n, 16), f32),
        dsc=((chunks, 128, 128), f32),
        h1=((rows_n, 128), f32),
        h2=((rows_n, 128), f32),
        db=((rows_n, 128), f32),
        dc=((rows_n, 128), f32),
        hs=((chunks, 8, 128), f32),
        gdt=((rows_n, 128), bf16),
        gbc=((rows_n, 256), bf16),
        ex_out=((BLOCKS, 8, WIDE), f32),
        ex_in=((BLOCKS, 8, WIDE), f32),
        eb_out=((8, 256), f32),
        eb_in=((8, 256), f32),)
    sems = dict(s_ss=(BLOCKS,), s_rs=(BLOCKS,), r_ss=(BLOCKS,), r_rs=(BLOCKS,), e_ss=(2,), e_rs=(2,))
    if direct:
        n, block = arrays["tokens"].shape[:2]
        scratch.update(iug=outs["iug"], odg=outs["odg"])
        outs = dict(
            out=((rows_n, d), bf16),
            tg_in=((n, block, d), bf16),
            all_up=((n, 16, d), bf16),
            all_rest=((BLOCKS, n, 16, d), bf16),
            all_end=((BLOCKS, n, 16, 256), bf16),
        )
        scratch.update(
            out_rows=((rows_n, d), bf16),
            tok_out=((n, block, d), bf16),
            ext=((rows_n + HALO, d), bf16),
            zx=((BLOCKS, d, 2 * WIDE), bf16),
            wout=((BLOCKS, d, WIDE), bf16),
            wbc=((d, 256), bf16),
            dts=((BLOCKS, n, 16, 128), bf16),
            wdt=((d, 128), bf16),
            up=((BLOCKS, 16, 2 * WIDE), bf16),
            small=((BLOCKS, 16, WIDE), f32),
            sum_out=((2, BLOCKS, 16, d), bf16),
            sum_in=((2, BLOCKS, 16, d), bf16),
            sum_all=((2, 16, d), bf16),
            end_out=((BLOCKS, 16, 256), bf16),
            end_in=((BLOCKS, 16, 256), bf16),
            end_all=((16, 256), bf16),
        )
        for name in LOADED:
            scratch["v_" + name] = (arrays[name].shape, arrays[name].dtype)
        pairs = dict(zx=(6, n), wo=(6, n), bc=(3, n), tok=(n,), dt=(n,), d2=(BLOCKS,), up=(BLOCKS,), sm=(BLOCKS,))
        pairs.update(ha=(1,), tg=(n,), ga=(BLOCKS,), gb=(BLOCKS,), gc=(n,), gd=(n,), g3=(BLOCKS,))
        pairs.update(ge=(BLOCKS,), gf=(n,), gg=(BLOCKS,))
        for name, shape in pairs.items():
            sems[name + "_ss"] = shape
            sems[name + "_rs"] = (BLOCKS, n) if name in ("zx", "wo") else shape[-1:]
        sems.update(own_sem=(7,), load_sem=(len(LOADED),))
    names = list(scalars) + list(arrays) + list(outs) + list(scratch) + list(sems)
    smem = pl.BlockSpec(memory_space=pltpu.SMEM)
    vmem = pl.BlockSpec(memory_space=pl.ANY if direct else pltpu.VMEM)
    results = pl.pallas_call(
        partial(mixer_kernel, direct, names),
        out_shape=[jax.ShapeDtypeStruct(*v) for v in outs.values()],
        in_specs=[smem] * len(scalars) + [vmem] * len(arrays),
        out_specs=[vmem] * len(outs),
        scratch_shapes=[pltpu.VMEM(*v) for v in scratch.values()]
        + [pltpu.SemaphoreType.DMA(n) for n in sems.values()],
        compiler_params=pltpu.CompilerParams(
            collective_id=1, has_side_effects=True, vmem_limit_bytes=63 * 1024 * 1024
        ),
    )(*scalars.values(), *arrays.values())
    return SimpleNamespace(**dict(zip(outs, results)))


def pack_small(x_kernel, x_offset, out_gain, dt_bias, a_log, d_skip):
    def block(v):
        return v.reshape(-1, BLOCKS, v.shape[-1] // BLOCKS).transpose(1, 0, 2)

    def heads(v):
        return jnp.pad(block(v[None]), ((0, 0), (0, 0), (0, WIDE - HEADS_B)))

    parts = [
        block(x_kernel),
        block(x_offset[None]),
        block(out_gain.astype(f32)[None]),
        heads(dt_bias),
        heads(a_log),
        heads(d_skip),
        jnp.zeros((BLOCKS, 7, WIDE), f32),
    ]
    return jnp.concatenate(parts, axis=1)


def shards(
    tokens,
    cotangent,
    lengths,
    dealt_to,
    adapter_id,
    norm_gain,
    w_zx,
    w_dt,
    w_bc,
    x_kernel,
    x_offset,
    bc_kernel,
    bc_offset,
    dt_bias,
    a_log,
    d_skip,
    out_gain,
    w_out,
    inlet_down,
    inlet_up,
    outlet_down,
    outlet_up,
):
    d = tokens.shape[3]
    tp_size, dp_size = lax.axis_size("tensor"), lax.axis_size("dp")
    if tp_size == BLOCKS and dp_size % 2 == 0 and w_bc.shape[0] % 16 == 0 and tokens.shape[2] * 2 <= CHUNK:
        n, block = tokens.shape[0], tokens.shape[2]
        res = mixer_call(
            True,
            dict(lengths=lengths, dealt_to=dealt_to, adapter_id=adapter_id),
            dict(
                tokens=tokens.reshape(n, block, d),
                cot=cotangent.reshape(-1, d),
                gain=norm_gain,
                w_zx=w_zx,
                w_out=w_out.T,
                w_bc=w_bc,
                w_dt_in=w_dt.T,
                x_kernel=x_kernel,
                x_offset=x_offset,
                out_gain=out_gain,
                dt_bias=dt_bias,
                a_log=a_log,
                d_skip=d_skip,
                bc_kernel=bc_kernel,
                bc_offset=bc_offset,
                inlet_down=inlet_down.transpose(0, 2, 1),
                inlet_up=inlet_up,
                outlet_down=outlet_down.transpose(0, 2, 1),
                outlet_up=outlet_up,
            ),
        )
        out, tok, idg, iug, odg, oug = settle_call(dealt_to, adapter_id, res)
        return (
            out.reshape(1, -1, d),
            tok.reshape(tokens.shape),
            idg.transpose(0, 2, 1),
            iug,
            odg.transpose(0, 2, 1),
            oug,
        )
    group_id, place = lax.axis_index("dp"), lax.axis_index("tensor")
    seq_count = dealt_to.shape[0]
    slots = jnp.arange(seq_count, dtype=jnp.int32)
    seq_of = jnp.sum((dealt_to[None, :] == slots[:, None]).astype(jnp.int32) * slots[None, :], axis=1)
    own = jnp.take(seq_of, group_id)
    adapter = jnp.take(adapter_id, own)
    chosen = (jnp.arange(inlet_down.shape[0], dtype=jnp.int32) == adapter).astype(f32)

    picked = jnp.take(tokens, seq_of, axis=0)
    tok = lax.all_to_all(picked, "dp", split_axis=0, concat_axis=2, tiled=True).reshape(-1, d)
    rows_n = tok.shape[0]
    ends = lax.ppermute(tok[-HALO:], "tensor", [(i, i + 1) for i in range(tp_size - 1)])
    ext = jnp.concatenate([ends, tok], axis=0)

    def both(v, axis_dp, axis_tp):
        v = lax.all_gather(v, "dp", axis=axis_dp, tiled=True)
        return lax.all_gather(v, "tensor", axis=axis_tp, tiled=True)

    full_zx = both(w_zx, 0, 2)
    full_out = both(w_out, 1, 0)
    full_dt = both(w_dt, 0, 1)
    full_bc = lax.all_gather(w_bc, "dp", axis=0, tiled=True)
    zx = full_zx.reshape(d, 2, BLOCKS, WIDE).transpose(2, 0, 1, 3).reshape(BLOCKS, d, 2 * WIDE)
    wout = full_out.T.reshape(d, BLOCKS, WIDE).transpose(1, 0, 2)
    wdt = jnp.pad(full_dt.reshape(d, BLOCKS, HEADS_B), ((0, 0), (0, 0), (0, SLOT - HEADS_B))).reshape(d, BLOCKS * SLOT)
    wdt = jnp.pad(wdt, ((0, 0), (0, 128 - BLOCKS * SLOT)))

    def over_tp(v):
        return lax.all_gather(v, "tensor", axis=v.ndim - 1, tiled=True)

    small = pack_small(*(over_tp(v) for v in (x_kernel, x_offset, out_gain, dt_bias, a_log, d_skip)))
    up = over_tp(jnp.take(inlet_up, adapter, axis=0))
    up = up.reshape(16, 2, BLOCKS, WIDE).transpose(2, 0, 1, 3).reshape(BLOCKS, 16, 2 * WIDE)

    res = mixer_call(
        False,
        dict(lengths=lengths, dealt_to=dealt_to, adapter_id=adapter_id),
        dict(
            ext=ext,
            cot=cotangent.reshape(rows_n, d),
            gain=norm_gain,
            zx=zx,
            wout=wout,
            wbc=full_bc,
            wdt=wdt,
            small=small,
            up=up,
            bc_kernel=bc_kernel,
            bc_offset=bc_offset,
            inlet_down=inlet_down.transpose(0, 2, 1),
            outlet_down=outlet_down.transpose(0, 2, 1),
            outlet_up=outlet_up,
        ),
    )
    output = res.out.reshape(1, rows_n, d)
    returned = lax.all_to_all(res.tg.reshape(1, 1, rows_n, d), "dp", split_axis=2, concat_axis=0, tiled=True)
    token_grads = jnp.take(returned, dealt_to, axis=0)
    pick = chosen[:, None, None]
    odg = res.odg.transpose(1, 0, 2).reshape(16, BLOCKS * WIDE)
    idg, odg, oug = lax.psum((pick * res.idg[None], pick * odg[None], pick * res.oug[None]), ("dp", "tensor"))
    iug = res.iug.reshape(BLOCKS, 16, 2, WIDE).transpose(1, 2, 0, 3).reshape(16, 2, BLOCKS * WIDE)
    iug = lax.psum_scatter(iug, "tensor", scatter_dimension=2, tiled=True)
    iug = lax.psum(pick[..., None] * iug[None], "dp")
    return (output, token_grads, idg.transpose(0, 2, 1), iug, odg.transpose(0, 2, 1), oug)


def solution(mesh):
    in_specs = (
        P(None, "tensor", "dp", None),
        P("dp", "tensor", None),
        P(),
        P(),
        P(),
        P(),
        P("dp", None, "tensor"),
        P("dp", "tensor"),
        P("dp", None),
        P(None, "tensor"),
        P("tensor"),
        P(),
        P(),
        P("tensor"),
        P("tensor"),
        P("tensor"),
        P("tensor"),
        P("tensor", "dp"),
        P(),
        P(None, None, None, "tensor"),
        P(),
        P(),
    )
    out_specs = (
        P("dp", "tensor", None),
        P(None, "tensor", "dp", None),
        P(),
        P(None, None, None, "tensor"),
        P(),
        P(),
    )
    return jax.shard_map(shards, mesh=mesh, in_specs=in_specs, out_specs=out_specs, check_vma=False)
```
